768 devices in a mesh: grp: 24 (over z, core), dev: 32 (over x, y).
Axes of the slice: x: 4, y: 8, z: 12, core: 2. Of those that a mesh axis runs over, the one named last changes fastest.
Arguments:
- tracer: float32 [72, 16, 98304], P(None, None, ('grp', 'dev')), may hold values from -6 to 6
- metric: float32 [98304], P(('grp', 'dev')), may hold values from 0.5 to 2
- coef: float32 [72, 1572864], P(None, ('grp', 'dev')), may hold values from 0.02 to 601
- nbr_slot: int32 [4, 98304], P(None, ('grp', 'dev')), may hold values from 0 to 559, as said below
- edge_flip: int32 [4, 98304], P(None, ('grp', 'dev')), may hold values from 0 to 1, as said below
- send_slot: int32 [36864], P(('grp', 'dev')), may hold values from 0 to 511, as said below
- span_slot: int32 [16, 98304], P(None, ('grp', 'dev')), may hold values from 0 to 65535, as said below
Outputs:
- mixed: float32 [72, 16, 98304], P(None, None, ('grp', 'dev'))
The draws below stay inside these ranges and needn't reach their ends.
Inputs may be any that keep to these rules, and one draw needn't show every extreme that they name: `nbr_slot`: entries below 512 name an edge of an element of the same device as s * 128 + e; larger ones name the neighbouring devices' buffer entries in the order of the edge table. Each element edge meets exactly one other edge, both ways. `edge_flip`: symmetric over the two sides of a shared edge. `send_slot`: each entry is an own edge s * 128 + e'. For each device, 16 own edges whose neighbours lie on device (g + 1, v), 16 for (g - 1, v), 8 for (g, v + 1), 8 for (g, v - 1), in the order the receiving edge table expects. `span_slot`: within each group along dev the values form a permutation of 0 to 65535, and every device holds exactly 64 columns whose value lies in each range r * 2048 to (r + 1) * 2048 - 1.
All inputs are finite; a program needn't handle non-finite values.
Results may differ from the reference program's by a relative error of at most 0.0003.
Values sent between devices are 32-bit elements; how exact they have to be, the bound alone decides.
No kernel may reach another device: no remote copies, remote signals or barrier semaphores. Data moves between devices by JAX's collectives and lax.ppermute only.
A program may use at most 32 MiB of HBM per device.

```python
import math
import jax
import jax.numpy as jnp
import numpy as np
from jax import lax

LEV = 72
BR = 8
BC = 16
E_DEV = 128
COLS_DEV = 2048
ELEMS = 98304
COLUMNS = 1572864
N_GRP = 24
N_DEV = 32


def block_geometry(key):
    devices = N_GRP * N_DEV
    rotation = jax.random.randint(jax.random.fold_in(key, 11), (N_GRP * BR, N_DEV * BC), 0, 4).astype(jnp.int32)
    dev_keys = jax.random.split(jax.random.fold_in(key, 12), devices)
    slot_pos = jax.vmap(lambda one_key: jax.random.permutation(one_key, E_DEV))(dev_keys).astype(jnp.int32)
    pos_slot = jnp.argsort(slot_pos, axis=1).astype(jnp.int32)
    dev_ids = jnp.arange(devices, dtype=jnp.int32)[:, None]
    return (rotation, slot_pos, pos_slot, dev_ids // N_DEV, dev_ids % N_DEV)


def neighbour_tables(key):
    rotation, slot_pos, pos_slot, grp_idx, dev_idx = block_geometry(key)
    grid_row = grp_idx * BR + slot_pos // BC
    grid_col = dev_idx * BC + slot_pos % BC
    turns = rotation[grid_row, grid_col]
    local_side = jnp.arange(4, dtype=jnp.int32)[:, None, None]
    facing = (local_side + turns[None]) % 4
    step_row = jnp.array([-1, 0, 1, 0], jnp.int32)[facing]
    step_col = jnp.array([0, 1, 0, -1], jnp.int32)[facing]
    next_row = (grid_row[None] + step_row) % (N_GRP * BR)
    next_col = (grid_col[None] + step_col) % (N_DEV * BC)
    next_dev = next_row // BR * N_DEV + next_col // BC
    in_row = next_row % BR
    in_col = next_col % BC
    next_slot = pos_slot[next_dev, in_row * BC + in_col]
    next_turns = rotation[next_row, next_col]
    next_side = (facing + 2 - next_turns) % 4
    home_dev = (grp_idx * N_DEV + dev_idx)[None]
    own_count = 4 * E_DEV
    remote = jnp.where(facing == 0, own_count + in_col, jnp.where(facing == 2, own_count + BC + in_col, jnp.where(facing == 3, own_count + 2 * BC + in_row, own_count + 2 * BC + BR + in_row)))
    slot_index = jnp.where(next_dev == home_dev, next_side * E_DEV + next_slot, remote)
    tangent_sign = jnp.array([[1, 1, -1, -1], [1, -1, -1, 1]], jnp.int32)
    flip_bits = (tangent_sign[local_side % 2, turns[None]] != tangent_sign[next_side % 2, next_turns]).astype(jnp.int32)
    return (slot_index.reshape(4, -1).astype(jnp.int32), flip_bits.reshape(4, -1))


def draw_nbr_slot(key, part):
    return neighbour_tables(key)[0]


def draw_edge_flip(key, part):
    return neighbour_tables(key)[1]


def draw_send_slot(key, part):
    rotation, slot_pos, pos_slot, grp_idx, dev_idx = block_geometry(key)

    def outward(rows_at, cols_at, facing):
        slot_here = pos_slot[:, rows_at * BC + cols_at]
        turns = rotation[grp_idx * BR + rows_at[None], dev_idx * BC + cols_at[None]]
        return (facing - turns) % 4 * E_DEV + slot_here
    along_cols = jnp.arange(BC, dtype=jnp.int32)
    along_rows = jnp.arange(BR, dtype=jnp.int32)
    pieces = [outward(BR - 1 + 0 * along_cols, along_cols, 2), outward(0 * along_cols, along_cols, 0), outward(along_rows, BC - 1 + 0 * along_rows, 1), outward(along_rows, 0 * along_rows, 3)]
    return jnp.concatenate(pieces, axis=1).reshape(-1).astype(jnp.int32)


def draw_span_slot(key, part):
    devices = N_GRP * N_DEV
    per_peer = COLS_DEV // N_DEV
    rank_keys = jax.random.split(jax.random.fold_in(key, 21), devices)
    place_keys = jax.random.split(jax.random.fold_in(key, 22), devices)
    ranks = jax.vmap(lambda one_key: jax.random.permutation(one_key, COLS_DEV))(rank_keys).astype(jnp.int32)
    arrivals = jax.vmap(lambda one_key: jax.random.permutation(one_key, COLS_DEV))(place_keys).astype(jnp.int32)
    dev_ids = jnp.arange(devices, dtype=jnp.int32)
    target = ranks // per_peer
    within = ranks % per_peer
    arrival_idx = (dev_ids % N_DEV)[:, None] * per_peer + within
    target_dev = (dev_ids // N_DEV)[:, None] * N_DEV + target
    position = arrivals[target_dev, arrival_idx]
    slot_value = target * COLS_DEV + position
    return slot_value.reshape(devices, 16, E_DEV).transpose(1, 0, 2).reshape(16, devices * E_DEV).astype(jnp.int32)


def draw_coef(key, part):
    column_key = jax.random.fold_in(key, 31)
    level_key = jax.random.fold_in(key, 32)
    level_factor = jnp.exp(jax.random.uniform(level_key, (LEV, COLUMNS), jnp.float32, -math.log(2.0), math.log(2.0)))
    column_scale = jnp.exp(jax.random.uniform(column_key, (COLUMNS,), jnp.float32, math.log(0.05), math.log(300.0)))
    return (column_scale[None, :] * level_factor).astype(jnp.float32)


def block_scale(stream_key, dims, cuts, smallest, high):
    def one(dim, parts):
        steps = jax.random.uniform(jax.random.fold_in(jax.random.fold_in(stream_key, 6), dim), (parts,), jnp.float32, smallest / len(cuts), high / len(cuts))
        return jnp.repeat(jnp.exp(steps), dims[dim] // parts).reshape((-1,) + (1,) * (len(dims) - dim - 1))

    loudness = one(*cuts[0])
    for cut in cuts[1:]:
        loudness = loudness * one(*cut)
    return loudness


def normal_values(stream_key, dims, scale, most, cuts=(), kind=jnp.bfloat16):
    factor_of = block_scale(stream_key, dims, cuts, -0.22, 0.18) if cuts else 1.0
    result = jax.random.normal(stream_key, dims, jnp.float32) * scale * factor_of
    return jnp.minimum(jnp.maximum(result, -most), most).astype(kind)


def setup_inputs(seed: int = 0) -> dict:
    key_list = jax.random.split(jax.random.key(seed), 8)
    return {
        "tracer": normal_values(key_list[0], (LEV, 16, ELEMS), 1.0, 6.0, ((2, 768),), jnp.float32),
        "metric": jnp.clip(jnp.exp(math.log(2.0) - 1.3862944 * jax.random.uniform(key_list[1], (ELEMS,), jnp.float32) ** block_scale(key_list[1], (ELEMS,), ((0, 768),), -0.2, 0.2)), 0.5, 2.0),
        "coef": draw_coef(jax.random.fold_in(key_list[7], 71), 0),
        "nbr_slot": draw_nbr_slot(jax.random.fold_in(key_list[7], 71), 0),
        "edge_flip": draw_edge_flip(jax.random.fold_in(key_list[7], 71), 0),
        "send_slot": draw_send_slot(jax.random.fold_in(key_list[7], 71), 0),
        "span_slot": draw_span_slot(jax.random.fold_in(key_list[7], 71), 0),
    }


PENALTY = 10.0
HYPER = 0.0001

def gll_tables():
    gll_nodes = np.array([-1.0, -1.0 / np.sqrt(5.0), 1.0 / np.sqrt(5.0), 1.0])
    weights = np.array([1.0 / 6.0, 5.0 / 6.0, 5.0 / 6.0, 1.0 / 6.0])
    lambdas = np.ones(4)
    for jdx in range(4):
        for kdx in range(4):
            if kdx != jdx:
                lambdas[jdx] = lambdas[jdx] / (gll_nodes[jdx] - gll_nodes[kdx])
    derivative = np.zeros((4, 4))
    for idx in range(4):
        for jdx in range(4):
            if idx != jdx:
                derivative[idx, jdx] = lambdas[jdx] / lambdas[idx] / (gll_nodes[idx] - gll_nodes[jdx])
        derivative[idx, idx] = -np.sum(derivative[idx])
    stiffness = -(derivative.T * weights[None, :] @ derivative) / weights[:, None]
    identity = np.eye(4)
    lap_matrix = np.kron(stiffness, identity) + np.kron(identity, stiffness)
    edge_points = np.array([[0, 1, 2, 3], [3, 7, 11, 15], [12, 13, 14, 15], [0, 4, 8, 12]])
    edge_order = edge_points.T.reshape(-1)
    spread = np.zeros((16, 16))
    spread[edge_order, np.arange(16)] = 1.0
    return (lap_matrix.astype(np.float32), spread.astype(np.float32), edge_order.astype(np.int32))

def own_traces(block_field):
    lap_matrix, spread, edge_order = gll_tables()
    levels, points, elem_count = block_field.shape
    return jnp.take(block_field, jnp.asarray(edge_order), axis=1).reshape(levels, 4, 4 * elem_count)

def element_operator(block_field, elem_scale, neighbours, flip_bits, incoming):
    lap_matrix, spread, edge_order = gll_tables()
    levels, points, elem_count = block_field.shape
    own_edges = own_traces(block_field)
    edge_table = jnp.concatenate([own_edges, incoming], axis=2)
    across = jnp.take(edge_table, neighbours, axis=2)
    across = jnp.where(flip_bits[None, None, :] == 1, across[:, ::-1, :], across)
    jump_terms = (PENALTY * (across - own_edges)).reshape(levels, 16, elem_count)
    inner_part = jnp.einsum('pq,lqe->lpe', jnp.asarray(lap_matrix), block_field, precision=lax.Precision.HIGHEST)
    edge_part = jnp.einsum('pk,lke->lpe', jnp.asarray(spread), jump_terms, precision=lax.Precision.HIGHEST)
    return elem_scale[None, None, :] * (inner_part + edge_part)

def apply_everywhere(fields, scales, neighbours, flip_bits, send_lists):
    levels = fields.shape[1]
    width = 2 * BC + 2 * BR

    def outgoing_of(bundle):
        return jnp.take(own_traces(bundle[0]), bundle[1], axis=2)
    outgoing = lax.map(outgoing_of, (fields, send_lists)).reshape(N_GRP, N_DEV, levels, 4, width)
    from_south = jnp.roll(outgoing[..., :BC], 1, axis=0)
    from_north = jnp.roll(outgoing[..., BC:2 * BC], -1, axis=0)
    from_west = jnp.roll(outgoing[..., 2 * BC:2 * BC + BR], 1, axis=1)
    from_east = jnp.roll(outgoing[..., 2 * BC + BR:], -1, axis=1)
    incoming = jnp.concatenate([from_south, from_north, from_west, from_east], axis=-1)
    incoming = incoming.reshape(N_GRP * N_DEV, levels, 4, width)

    def operate_one(bundle):
        return element_operator(bundle[0], bundle[1], bundle[2], bundle[3], bundle[4])
    return lax.map(operate_one, (fields, scales, neighbours, flip_bits, incoming))

def vertical_solve(values, mixing):
    columns = values.shape[1]
    mixing_below = jnp.concatenate([mixing[1:], jnp.zeros((1, columns), jnp.float32)], axis=0)
    diagonal = 1.0 + mixing + mixing_below
    sub_diag = jnp.concatenate([jnp.zeros((1, columns), jnp.float32), -mixing[1:]], axis=0)
    super_diag = -mixing_below

    def forward(carry, level_in):
        upper_prev, rhs_prev = carry
        sub_here, diag_here, sup_here, rhs_here = level_in
        denom = diag_here - sub_here * upper_prev
        upper_now = sup_here / denom
        rhs_now = (rhs_here - sub_here * rhs_prev) / denom
        return ((upper_now, rhs_now), (upper_now, rhs_now))
    start = (jnp.zeros((columns,), jnp.float32), jnp.zeros((columns,), jnp.float32))
    ignored, (uppers, rhs_mod) = lax.scan(forward, start, (sub_diag, diagonal, super_diag, values))

    def backward(below, level_in):
        upper_here, rhs_here = level_in
        solved_here = rhs_here - upper_here * below
        return (solved_here, solved_here)
    ignored_too, solved = lax.scan(backward, jnp.zeros((columns,), jnp.float32), (uppers, rhs_mod), reverse=True)
    return solved

def reference(tracer, metric, coef, nbr_slot, edge_flip, send_slot, span_slot):
    devices = N_GRP * N_DEV
    fields = tracer.reshape(LEV, 16, devices, E_DEV).transpose(2, 0, 1, 3)
    scales = metric.reshape(devices, E_DEV)
    neighbours = nbr_slot.reshape(4, devices, E_DEV).transpose(1, 0, 2).reshape(devices, 4 * E_DEV)
    flip_bits = edge_flip.reshape(4, devices, E_DEV).transpose(1, 0, 2).reshape(devices, 4 * E_DEV)
    send_lists = send_slot.reshape(devices, 2 * BC + 2 * BR)
    first_pass = apply_everywhere(fields, scales, neighbours, flip_bits, send_lists)
    second = apply_everywhere(first_pass, scales, neighbours, flip_bits, send_lists)
    stepped = fields - HYPER * second
    span_ids = span_slot.reshape(16, devices, E_DEV).transpose(1, 0, 2).reshape(devices, 16 * E_DEV)
    offsets = jnp.arange(devices, dtype=jnp.int32) // N_DEV * (N_DEV * COLS_DEV)
    sources = (span_ids + offsets[:, None]).astype(jnp.int32)

    def column_step(bundle):
        mixing = jnp.take(coef, bundle[1], axis=1)
        return vertical_solve(bundle[0].reshape(LEV, COLS_DEV), mixing)
    mixed_out = lax.map(column_step, (stepped, sources))
    return mixed_out.reshape(devices, LEV, 16, E_DEV).transpose(1, 2, 0, 3).reshape(LEV, 16, devices * E_DEV)
```

```python
import jax
import jax.numpy as jnp
import numpy as np
from jax import lax
from jax.experimental import pallas as pl
from jax.experimental.pallas import tpu as pltpu
from jax.sharding import PartitionSpec as P

BR = 8
BC = 16
LEV = 72
PTS = 16
ELEM = 128
COLS = PTS * ELEM
PEERS = 32
PER = COLS // PEERS
ROWS = 40
BLOCKS = LEV // 8

PENALTY = 10.0
HYPER = 0.0001

VMEM = pl.BlockSpec(memory_space=pltpu.VMEM)
SMEM = pl.BlockSpec(memory_space=pltpu.SMEM)
PARAMS = pltpu.CompilerParams(vmem_limit_bytes=8 << 20)

EDGE_POINT = [[0, 1, 2, 3], [3, 7, 11, 15], [12, 13, 14, 15], [0, 4, 8, 12]]


def stiffness():
    nodes = np.array([-1.0, -1.0 / np.sqrt(5.0), 1.0 / np.sqrt(5.0), 1.0])
    weights = np.array([1.0 / 6.0, 5.0 / 6.0, 5.0 / 6.0, 1.0 / 6.0])
    lambdas = np.ones(4)
    for j in range(4):
        for k in range(4):
            if k != j:
                lambdas[j] = lambdas[j] / (nodes[j] - nodes[k])
    deriv = np.zeros((4, 4))
    for i in range(4):
        for j in range(4):
            if i != j:
                deriv[i, j] = lambdas[j] / lambdas[i] / (nodes[i] - nodes[j])
        deriv[i, i] = -np.sum(deriv[i])
    return -(deriv.T * weights[None, :] @ deriv) / weights[:, None]


def iota(shape, dim):
    return lax.broadcasted_iota(jnp.int32, shape, dim)


def parts_of(value):
    high = value.astype(jnp.bfloat16)
    low = (value - high.astype(jnp.float32)).astype(jnp.bfloat16)
    return jnp.concatenate([high, low], axis=0)


def moved(stacked, hot):
    product = jnp.dot(stacked, hot, preferred_element_type=jnp.float32)
    half = product.shape[0] // 2
    return product[:half] + product[half:]


def one_hot(index, depth):
    width = index.shape[1]
    low, high = index & (ELEM - 1), index >> 7
    base = jnp.broadcast_to(low, (ELEM, width)) == iota((ELEM, width), 0)
    base = jnp.where(base, 1.0, 0.0).astype(jnp.bfloat16)
    return jnp.concatenate(
        [
            base * jnp.broadcast_to(jnp.where(high == h, 1.0, 0.0), (ELEM, width)).astype(jnp.bfloat16)
            for h in range(depth // ELEM)
        ],
        axis=0,
    )


def inside(value):
    return pltpu.with_memory_space_constraint(value, pltpu.VMEM)


def route_kernel(span_ref, req_ref, bucket_ref):
    span = span_ref[...]
    target = span >> 11
    pos = span & (COLS - 1)
    peer = iota((PEERS, ELEM), 0)
    hot = [
        jnp.where(jnp.broadcast_to(target[p : p + 1], (PEERS, ELEM)) == peer, 1.0, 0.0)
        for p in range(PTS)
    ]
    stacked = jnp.concatenate(hot, axis=0).astype(jnp.bfloat16)
    row, col = iota((ELEM, 2 * ELEM), 0), iota((ELEM, 2 * ELEM), 1)
    ahead = jnp.where((row < col) | (col >= ELEM), 1.0, 0.0).astype(jnp.bfloat16)
    counts = jnp.dot(stacked, ahead, preferred_element_type=jnp.float32)
    base = jnp.zeros((PEERS, ELEM), jnp.float32)
    arrivals = []
    for p in range(PTS):
        here = counts[p * PEERS : (p + 1) * PEERS]
        arrivals.append(jnp.sum(hot[p] * (here[:, :ELEM] + base), axis=0, keepdims=True))
        base = base + here[:, ELEM:]
    arrival = jnp.concatenate(arrivals, axis=0).astype(jnp.int32)
    bucket_ref[...] = target * PER + arrival
    high = (pos >> 8).astype(jnp.float32)
    low = (pos & 255).astype(jnp.float32)
    slot = iota((PER, ELEM), 0)
    left, right = [], []
    for p in range(PTS):
        left.append(
            jnp.concatenate([hot[p] * high[p : p + 1], hot[p] * low[p : p + 1]], axis=0)
        )
        right.append(
            jnp.where(jnp.broadcast_to(arrival[p : p + 1], (PER, ELEM)) == slot, 1.0, 0.0)
        )
    left = jnp.concatenate(left, axis=1).astype(jnp.bfloat16)
    right = jnp.concatenate(right, axis=1).astype(jnp.bfloat16)
    right = jnp.concatenate([right, right], axis=0)
    parts = lax.dot_general(
        left, right, (((1,), (1,)), ((), ())), preferred_element_type=jnp.float32
    )
    asked = (parts[:PEERS] * 256.0 + parts[PEERS:]).astype(jnp.int32)
    for r in range(PEERS):
        req_ref[r] = asked[r : r + 1]


def route(span_slot):
    return pl.pallas_call(
        route_kernel,
        out_shape=(
            pltpu.VMEM((PEERS, 1, ELEM), jnp.int32),
            pltpu.VMEM((PTS, ELEM), jnp.int32),
        ),
        in_specs=[VMEM],
        out_specs=(VMEM, VMEM),
        compiler_params=PARAMS,
        name="route",
    )(span_slot)


def reply_kernel(coef_ref, got_ref, out_ref, data):
    data[...] = parts_of(coef_ref[...])
    lane = iota((1, ELEM), 1)
    first_half = iota((8, ELEM), 1) < PER
    for pair in range(PTS // 2):
        chunks = (2 * pair, 2 * pair + 1)
        asked = [jnp.where(lane < PER, got_ref[2 * c], got_ref[2 * c + 1]) for c in chunks]
        value = moved(data[...], one_hot(jnp.concatenate(asked, axis=1), COLS))
        for u, c in enumerate(chunks):
            acc = [value[8 * b : 8 * b + 8, u * ELEM : (u + 1) * ELEM] for b in range(BLOCKS)]
            turned = [pltpu.roll(block, PER, 1) for block in acc]
            for b in range(5):
                upper = 5 + b if b < 4 else b
                at = slice(8 * b, 8 * b + 8)
                out_ref[2 * c, at, :] = jnp.where(first_half, acc[b], turned[upper])
                out_ref[2 * c + 1, at, :] = jnp.where(first_half, turned[b], acc[upper])


def reply(coef, got):
    return pl.pallas_call(
        reply_kernel,
        out_shape=pltpu.VMEM((PEERS, ROWS, ELEM), jnp.float32),
        in_specs=[VMEM, VMEM],
        out_specs=VMEM,
        scratch_shapes=[pltpu.VMEM((2 * LEV, COLS), jnp.bfloat16)],
        compiler_params=PARAMS,
        name="reply",
    )(inside(coef), inside(got))


TABLE = 5 * ELEM


def send_lanes(send_ref):
    lane = iota((1, ELEM), 1)
    chosen = jnp.full((1, ELEM), 4 * ELEM, jnp.int32)
    for i in range(2 * BC + 2 * BR):
        chosen = jnp.where(lane == i, send_ref[i], chosen)
    return chosen


def fill_edges(edges, point):
    for t in range(4):
        for s in range(4):
            edges[t * LEV : (t + 1) * LEV, s * ELEM : (s + 1) * ELEM] = point(EDGE_POINT[s][t])


def emit(edges, send_ref, row_ref, col_ref):
    out = moved(parts_of(edges[:, : 4 * ELEM]), one_hot(send_lanes(send_ref), 4 * ELEM))
    lane = iota((LEV, ELEM), 1)
    for t in range(4):
        here = out[t * LEV : (t + 1) * LEV]
        row = here if t == 0 else pltpu.roll(here, 32 * t, 1)
        col = pltpu.roll(here, ELEM - 32 + 16 * t, 1)
        row_out = row if t == 0 else jnp.where((lane >> 5) == t, row, row_out)
        col_out = col if t == 0 else jnp.where((lane >> 4) == t, col, col_out)
    row_ref[...] = row_out
    col_ref[...] = col_out


def halo_kernel(tracer_ref, send_ref, row_ref, col_ref, edges):
    fill_edges(edges, lambda p: tracer_ref[pl.ds(p, LEV, stride=PTS), :])
    emit(edges, send_ref, row_ref, col_ref)


FLAT = pltpu.VMEM((LEV, ELEM), jnp.float32)


def halo(tracer, send_slot):
    return pl.pallas_call(
        halo_kernel,
        out_shape=(FLAT, FLAT),
        in_specs=[VMEM, SMEM],
        out_specs=(VMEM, VMEM),
        scratch_shapes=[pltpu.VMEM((4 * LEV, 4 * ELEM), jnp.float32)],
        compiler_params=PARAMS,
        name="halo",
    )(inside(tracer), send_slot)


def gather_across(edges, across, nbr_ref, incoming):
    lane = iota((LEV, ELEM), 1)
    below, above, west, east = [ref[...] for ref in incoming]
    row_in = jnp.where((lane & 31) < BC, below, above)
    col_in = jnp.where((lane & 15) < BR, west, east)
    for t in range(4):
        row = row_in if t == 0 else pltpu.roll(row_in, ELEM - 32 * t, 1)
        col = pltpu.roll(col_in, 32 if t < 1 else (ELEM + 32 - 16 * t) % ELEM, 1) if t != 2 else col_in
        edges[t * LEV : (t + 1) * LEV, 4 * ELEM :] = jnp.where(lane < 32, row, col)
    index = jnp.concatenate([nbr_ref[s : s + 1, :] for s in range(4)], axis=1)
    across[...] = moved(parts_of(edges[...]), one_hot(index, TABLE))


def operator(slabs, metric, turned, across, b):
    stiff = stiffness()
    edge_sum = [None] * PTS
    for s in range(4):
        raw = [
            across[pl.ds(pl.multiple_of(t * LEV + b * 8, 8), 8), s * ELEM : (s + 1) * ELEM]
            for t in range(4)
        ]
        for t in range(4):
            p = EDGE_POINT[s][t]
            value = jnp.where(turned[s], raw[3 - t], raw[t])
            edge_sum[p] = value if edge_sum[p] is None else edge_sum[p] + value
    result = []
    for i in range(4):
        for j in range(4):
            p = 4 * i + j
            edges = (i in (0, 3)) + (j in (0, 3))
            total = slabs[p] * float(stiff[i, i] + stiff[j, j] - PENALTY * edges)
            for q in range(4):
                if q != i:
                    total = total + slabs[4 * q + j] * float(stiff[i, q])
                if q != j:
                    total = total + slabs[4 * i + q] * float(stiff[j, q])
            if edges:
                total = total + PENALTY * edge_sum[p]
            result.append(metric * total)
    return result


def turned_of(flip_ref):
    return [jnp.broadcast_to(flip_ref[s : s + 1, :], (8, ELEM)) == 1 for s in range(4)]


def first_kernel(
    tracer_ref, metric_ref, nbr_ref, flip_ref, send_ref, below_ref, above_ref, west_ref, east_ref,
    first_ref, row_ref, col_ref, edges, across,
):
    fill_edges(edges, lambda p: tracer_ref[pl.ds(p, LEV, stride=PTS), :])
    gather_across(edges, across, nbr_ref, (below_ref, above_ref, west_ref, east_ref))
    metric = jnp.broadcast_to(metric_ref[...], (8, ELEM))

    def block(b, carry):
        at = pl.ds(pl.multiple_of(b * 8, 8), 8)
        slabs = [tracer_ref[pl.ds(b * (8 * PTS) + p, 8, stride=PTS), :] for p in range(PTS)]
        result = operator(slabs, metric, turned_of(flip_ref), across, b)
        for p in range(PTS):
            first_ref[p, at, :] = result[p]
        return carry

    lax.fori_loop(0, BLOCKS, block, 0)
    fill_edges(edges, lambda p: first_ref[p])
    emit(edges, send_ref, row_ref, col_ref)


EDGE_SCRATCH = [
    pltpu.VMEM((4 * LEV, TABLE), jnp.float32),
    pltpu.VMEM((4 * LEV, 4 * ELEM), jnp.float32),
]


def first_pass(tracer, metric, nbr, flip, send_slot, incoming):
    return pl.pallas_call(
        first_kernel,
        out_shape=(pltpu.VMEM((PTS, LEV, ELEM), jnp.float32), FLAT, FLAT),
        in_specs=[VMEM, VMEM, VMEM, VMEM, SMEM] + [VMEM] * 4,
        out_specs=(VMEM, VMEM, VMEM),
        scratch_shapes=EDGE_SCRATCH,
        compiler_params=PARAMS,
        name="first_pass",
    )(inside(tracer), metric, nbr, flip, send_slot, *[inside(x) for x in incoming])


def second_kernel(
    tracer_ref, field_ref, metric_ref, nbr_ref, flip_ref, below_ref, above_ref, west_ref, east_ref,
    stepped_ref, edges, across,
):
    fill_edges(edges, lambda p: field_ref[p])
    gather_across(edges, across, nbr_ref, (below_ref, above_ref, west_ref, east_ref))
    metric = jnp.broadcast_to(metric_ref[...], (8, ELEM))

    def block(b, carry):
        at = pl.ds(pl.multiple_of(b * 8, 8), 8)
        slabs = [field_ref[p, at, :] for p in range(PTS)]
        result = operator(slabs, metric, turned_of(flip_ref), across, b)
        for p in range(PTS):
            point = pl.ds(b * (8 * PTS) + p, 8, stride=PTS)
            stepped_ref[point, :] = tracer_ref[point, :] - HYPER * result[p]
        return carry

    lax.fori_loop(0, BLOCKS, block, 0)


def second_pass(tracer, field, metric, nbr, flip, incoming):
    return pl.pallas_call(
        second_kernel,
        out_shape=pltpu.VMEM((LEV * PTS, ELEM), jnp.float32),
        in_specs=[VMEM] * 9,
        out_specs=VMEM,
        scratch_shapes=EDGE_SCRATCH,
        compiler_params=PARAMS,
        name="second_pass",
    )(inside(tracer), inside(field), metric, nbr, flip, *[inside(x) for x in incoming])


def mix_kernel(reply_ref, bucket_ref, stepped_ref, out_ref, wide, data, mixing, gain, carried):
    first_half = iota((8, ELEM), 1) < PER
    for c in range(PTS):
        lanes = slice(c * ELEM, (c + 1) * ELEM)
        even = [reply_ref[2 * c, 8 * b : 8 * b + 8, :] for b in range(5)]
        odd = [reply_ref[2 * c + 1, 8 * b : 8 * b + 8, :] for b in range(5)]
        for b in range(5):
            wide[8 * b : 8 * b + 8, lanes] = jnp.where(
                first_half, even[b], pltpu.roll(odd[b], PER, 1)
            )
        for b in range(4):
            wide[40 + 8 * b : 48 + 8 * b, lanes] = jnp.where(
                first_half, pltpu.roll(even[b], PER, 1), odd[b]
            )
    data[...] = parts_of(wide[...])
    for p in range(0, PTS, 2):
        index = jnp.concatenate([bucket_ref[p : p + 1, :], bucket_ref[p + 1 : p + 2, :]], axis=1)
        value = moved(data[...], one_hot(index, COLS))
        for u in range(2):
            mixing[pl.ds(p + u, LEV, stride=PTS), :] = value[:, u * ELEM : (u + 1) * ELEM]

    def level(ref, k):
        return ref[k * PTS : (k + 1) * PTS, :]

    zero = jnp.zeros((PTS, ELEM), jnp.float32)
    half = LEV // 2
    up_gain, up_rhs, down_gain, down_rhs = zero, zero, zero, zero
    for i in range(half):
        k = i
        here, after = level(mixing, k), level(mixing, k + 1)
        scale = 1.0 / (1.0 + after + here * (1.0 - up_gain))
        up_rhs = (level(stepped_ref, k) + here * up_rhs) * scale
        up_gain = after * scale
        if i < half - 1:
            gain[k * PTS : (k + 1) * PTS, :] = up_gain
            carried[k * PTS : (k + 1) * PTS, :] = up_rhs
        m = LEV - 1 - i
        here = level(mixing, m)
        after = zero if i == 0 else level(mixing, m + 1)
        scale = 1.0 / (1.0 + here + after * (1.0 - down_gain))
        down_rhs = (level(stepped_ref, m) + after * down_rhs) * scale
        down_gain = here * scale
        if i < half - 1:
            gain[m * PTS : (m + 1) * PTS, :] = down_gain
            carried[m * PTS : (m + 1) * PTS, :] = down_rhs
    upper = (up_rhs + up_gain * down_rhs) / (1.0 - up_gain * down_gain)
    lower = down_rhs + down_gain * upper
    out_ref[half - 1] = upper
    out_ref[half] = lower
    for i in range(half - 2, -1, -1):
        upper = level(carried, i) + level(gain, i) * upper
        out_ref[i] = upper
        m = LEV - 1 - i
        lower = level(carried, m) + level(gain, m) * lower
        out_ref[m] = lower


def mix(replied, bucket, stepped):
    rows = LEV * PTS
    return pl.pallas_call(
        mix_kernel,
        out_shape=jax.ShapeDtypeStruct((LEV, PTS, ELEM), jnp.float32),
        in_specs=[VMEM] * 3,
        out_specs=VMEM,
        scratch_shapes=[
            pltpu.VMEM((LEV, COLS), jnp.float32),
            pltpu.VMEM((2 * LEV, COLS), jnp.bfloat16),
            pltpu.VMEM((rows, ELEM), jnp.float32),
            pltpu.VMEM((rows, ELEM), jnp.float32),
            pltpu.VMEM((rows, ELEM), jnp.float32),
        ],
        compiler_params=PARAMS,
        name="mix",
    )(inside(replied), inside(bucket), inside(stepped))


def exchange(row_out, col_out):
    def both(value, axis):
        size = lax.axis_size(axis)
        up = [(i, (i + 1) % size) for i in range(size)]
        down = [(j, i) for i, j in up]
        return lax.ppermute(value, axis, up), lax.ppermute(value, axis, down)

    return both(row_out, "grp") + both(col_out, "dev")


def on_device(tracer, metric, coef, nbr_slot, edge_flip, send_slot, span_slot):
    flat = tracer.reshape(LEV * PTS, ELEM)
    metric = metric.reshape(1, ELEM)
    asked, bucket = route(span_slot)
    got = lax.all_to_all(asked, "dev", split_axis=0, concat_axis=0, tiled=True)
    row_out, col_out = halo(flat, send_slot)
    got, row_out, col_out = lax.optimization_barrier((got, row_out, col_out))
    incoming = exchange(row_out, col_out)
    replied = lax.all_to_all(reply(coef, got), "dev", split_axis=0, concat_axis=0, tiled=True)
    first, row_out, col_out = first_pass(flat, metric, nbr_slot, edge_flip, send_slot, incoming)
    stepped = second_pass(flat, first, metric, nbr_slot, edge_flip, exchange(row_out, col_out))
    return mix(replied, bucket, stepped)


def solution(mesh):
    in_specs = (
        P(None, None, ("grp", "dev")),
        P(("grp", "dev")),
        P(None, ("grp", "dev")),
        P(None, ("grp", "dev")),
        P(None, ("grp", "dev")),
        P(("grp", "dev")),
        P(None, ("grp", "dev")),
    )
    out_specs = P(None, None, ("grp", "dev"))
    return jax.shard_map(
        on_device, mesh=mesh, in_specs=in_specs, out_specs=out_specs, check_vma=False
    )
```

```python
import jax
import jax.numpy as jnp
import numpy as np
from jax import lax
from jax.experimental import pallas as pl
from jax.experimental.pallas import tpu as pltpu
from jax.sharding import PartitionSpec as P

BR = 8
BC = 16
LEV = 72
PTS = 16
ELEM = 128
COLS = PTS * ELEM
PEERS = 32
PER = COLS // PEERS
BLOCKS = LEV // 8
SCALE = 5

PENALTY = 10.0
HYPER = 0.0001

VMEM = pl.BlockSpec(memory_space=pltpu.VMEM)
PARAMS = pltpu.CompilerParams(vmem_limit_bytes=8 << 20)

EDGE_POINT = [[0, 1, 2, 3], [3, 7, 11, 15], [12, 13, 14, 15], [0, 4, 8, 12]]


def stiffness():
    nodes = np.array([-1.0, -1.0 / np.sqrt(5.0), 1.0 / np.sqrt(5.0), 1.0])
    weights = np.array([1.0 / 6.0, 5.0 / 6.0, 5.0 / 6.0, 1.0 / 6.0])
    lambdas = np.ones(4)
    for j in range(4):
        for k in range(4):
            if k != j:
                lambdas[j] = lambdas[j] / (nodes[j] - nodes[k])
    deriv = np.zeros((4, 4))
    for i in range(4):
        for j in range(4):
            if i != j:
                deriv[i, j] = lambdas[j] / lambdas[i] / (nodes[i] - nodes[j])
        deriv[i, i] = -np.sum(deriv[i])
    return -(deriv.T * weights[None, :] @ deriv) / weights[:, None]


def iota(shape, dim):
    return lax.broadcasted_iota(jnp.int32, shape, dim)


def outside(value):
    return pltpu.with_memory_space_constraint(value, pltpu.HBM)


def parts_of(value):
    high = value.astype(jnp.bfloat16)
    low = (value - high.astype(jnp.float32)).astype(jnp.bfloat16)
    return jnp.concatenate([high, low], axis=0)


def moved(stacked, hot):
    product = jnp.dot(stacked, hot, preferred_element_type=jnp.float32)
    half = product.shape[0] // 2
    return product[:half] + product[half:]


def one_hot(index, depth):
    width = index.shape[1]
    low, high = index & (ELEM - 1), index >> 7
    base = jnp.broadcast_to(low, (ELEM, width)) == iota((ELEM, width), 0)
    base = jnp.where(base, 1.0, 0.0).astype(jnp.bfloat16)
    return jnp.concatenate(
        [
            base * jnp.broadcast_to(jnp.where(high == h, 1.0, 0.0), (ELEM, width)).astype(jnp.bfloat16)
            for h in range(depth // ELEM)
        ],
        axis=0,
    )


def cost(micros):
    work = int(SCALE * micros * 1e9)
    return pl.CostEstimate(flops=work, bytes_accessed=1 << 20, transcendentals=0)


def inside(value):
    return pltpu.with_memory_space_constraint(value, pltpu.VMEM)


def route_kernel(
    span_ref, nbr_ref, flip_ref, send_ref, metric_ref, req_ref, bucket_ref, table_ref, scale_ref
):
    table_ref[0:4, :] = nbr_ref[...]
    table_ref[4:8, :] = flip_ref[...]
    table_ref[8:16, :] = jnp.full((8, ELEM), 4 * ELEM, jnp.int32)
    table_ref[8:9, : 2 * BC + 2 * BR] = send_ref[...]
    scale_ref[...] = jnp.broadcast_to(metric_ref[...], (8, ELEM))
    span = span_ref[...]
    target = span >> 11
    pos = span & (COLS - 1)
    peer = iota((PEERS, ELEM), 0)
    hot = [
        jnp.where(jnp.broadcast_to(target[p : p + 1], (PEERS, ELEM)) == peer, 1.0, 0.0)
        for p in range(PTS)
    ]
    stacked = jnp.concatenate(hot, axis=0).astype(jnp.bfloat16)
    row, col = iota((ELEM, 2 * ELEM), 0), iota((ELEM, 2 * ELEM), 1)
    ahead = jnp.where((row < col) | (col >= ELEM), 1.0, 0.0).astype(jnp.bfloat16)
    counts = jnp.dot(stacked, ahead, preferred_element_type=jnp.float32)
    base = jnp.zeros((PEERS, ELEM), jnp.float32)
    arrivals = []
    for p in range(PTS):
        here = counts[p * PEERS : (p + 1) * PEERS]
        arrivals.append(jnp.sum(hot[p] * (here[:, :ELEM] + base), axis=0, keepdims=True))
        base = base + here[:, ELEM:]
    arrival = jnp.concatenate(arrivals, axis=0).astype(jnp.int32)
    bucket_ref[...] = target * PER + arrival
    high = (pos >> 8).astype(jnp.float32)
    low = (pos & 255).astype(jnp.float32)
    slot = iota((PER, ELEM), 0)
    left, right = [], []
    for p in range(PTS):
        left.append(
            jnp.concatenate([hot[p] * high[p : p + 1], hot[p] * low[p : p + 1]], axis=0)
        )
        right.append(
            jnp.where(jnp.broadcast_to(arrival[p : p + 1], (PER, ELEM)) == slot, 1.0, 0.0)
        )
    left = jnp.concatenate(left, axis=1).astype(jnp.bfloat16)
    right = jnp.concatenate(right, axis=1).astype(jnp.bfloat16)
    right = jnp.concatenate([right, right], axis=0)
    parts = lax.dot_general(
        left, right, (((1,), (1,)), ((), ())), preferred_element_type=jnp.float32
    )
    asked = (parts[:PEERS] * 256.0 + parts[PEERS:]).astype(jnp.int32)
    for r in range(PEERS):
        req_ref[r] = asked[r : r + 1]


def reply_kernel(coef_ref, got_ref, out_ref, data):
    data[...] = parts_of(coef_ref[...])
    lane = iota((1, ELEM), 1)
    first_half = iota((8, ELEM), 1) < PER
    for pair in range(PTS // 2):
        chunks = (2 * pair, 2 * pair + 1)
        asked = [jnp.where(lane < PER, got_ref[2 * c], got_ref[2 * c + 1]) for c in chunks]
        value = moved(data[...], one_hot(jnp.concatenate(asked, axis=1), COLS))
        for u, c in enumerate(chunks):
            acc = [value[8 * b : 8 * b + 8, u * ELEM : (u + 1) * ELEM] for b in range(BLOCKS)]
            for b in range(BLOCKS):
                turned = pltpu.roll(acc[b], PER, 1)
                even = jnp.where(first_half, acc[b], pltpu.roll(turned, 4, 0))
                odd = jnp.where(first_half, turned, pltpu.roll(acc[b], 4, 0))
                out_ref[2 * c, b] = even[:4]
                out_ref[2 * c + 1, b] = odd[:4]


def reply(coef, got):
    return pl.pallas_call(
        reply_kernel,
        out_shape=pltpu.VMEM((PEERS, BLOCKS, 4, ELEM), jnp.float32),
        in_specs=[VMEM, VMEM],
        out_specs=VMEM,
        scratch_shapes=[pltpu.VMEM((2 * LEV, COLS), jnp.bfloat16)],
        compiler_params=PARAMS,
        cost_estimate=cost(2.4),
        name="reply",
    )(inside(coef), inside(got))


TABLE = 5 * ELEM


def fill_edges(edges, point):
    for t in range(4):
        for s in range(4):
            edges[t * LEV : (t + 1) * LEV, s * ELEM : (s + 1) * ELEM] = point(EDGE_POINT[s][t])


def emit(edges, chosen, row_ref, col_ref):
    out = moved(parts_of(edges[:, : 4 * ELEM]), one_hot(chosen, 4 * ELEM))
    lane = iota((LEV, ELEM), 1)
    for t in range(4):
        here = out[t * LEV : (t + 1) * LEV]
        row = here if t == 0 else pltpu.roll(here, 32 * t, 1)
        col = pltpu.roll(here, ELEM - 32 + 16 * t, 1)
        row_out = row if t == 0 else jnp.where((lane >> 5) == t, row, row_out)
        col_out = col if t == 0 else jnp.where((lane >> 4) == t, col, col_out)
    row_ref[...] = row_out
    col_ref[...] = col_out


FLAT = pltpu.VMEM((LEV, ELEM), jnp.float32)


def route(span_slot, nbr_slot, edge_flip, send_slot, metric):
    return pl.pallas_call(
        route_kernel,
        out_shape=(
            pltpu.VMEM((PEERS, 1, ELEM), jnp.int32),
            pltpu.VMEM((PTS, ELEM), jnp.int32),
            pltpu.VMEM((16, ELEM), jnp.int32),
            pltpu.VMEM((8, ELEM), jnp.float32),
        ),
        in_specs=[VMEM] * 5,
        out_specs=(VMEM,) * 4,
        compiler_params=PARAMS,
        cost_estimate=cost(1.2),
        name="route",
    )(*[outside(x) for x in (span_slot, nbr_slot, edge_flip, send_slot.reshape(1, -1), metric.reshape(1, ELEM))])


def halo_kernel(tracer_ref, table_ref, row_ref, col_ref, edges):
    fill_edges(edges, lambda p: tracer_ref[pl.ds(p, LEV, stride=PTS), :])
    emit(edges, table_ref[8:9, :], row_ref, col_ref)


def halo(tracer, table):
    return pl.pallas_call(
        halo_kernel,
        out_shape=(FLAT, FLAT),
        in_specs=[VMEM, VMEM],
        out_specs=(VMEM, VMEM),
        scratch_shapes=[pltpu.VMEM((4 * LEV, 4 * ELEM), jnp.float32)],
        compiler_params=PARAMS,
        cost_estimate=cost(1.0),
        name="halo",
    )(inside(tracer), inside(table))


def gather_across(edges, across, table_ref, incoming):
    lane = iota((LEV, ELEM), 1)
    below, above, west, east = [ref[...] for ref in incoming]
    row_in = jnp.where((lane & 31) < BC, below, above)
    col_in = jnp.where((lane & 15) < BR, west, east)
    for t in range(4):
        row = row_in if t == 0 else pltpu.roll(row_in, ELEM - 32 * t, 1)
        col = pltpu.roll(col_in, 32 if t < 1 else (ELEM + 32 - 16 * t) % ELEM, 1) if t != 2 else col_in
        edges[t * LEV : (t + 1) * LEV, 4 * ELEM :] = jnp.where(lane < 32, row, col)
    index = jnp.concatenate([table_ref[s : s + 1, :] for s in range(4)], axis=1)
    across[...] = moved(parts_of(edges[...]), one_hot(index, TABLE))


def operator(slabs, metric, turned, across, b):
    stiff = stiffness()
    edge_sum = [None] * PTS
    for s in range(4):
        raw = [
            across[pl.ds(pl.multiple_of(t * LEV + b * 8, 8), 8), s * ELEM : (s + 1) * ELEM]
            for t in range(4)
        ]
        for t in range(4):
            p = EDGE_POINT[s][t]
            value = jnp.where(turned[s], raw[3 - t], raw[t])
            edge_sum[p] = value if edge_sum[p] is None else edge_sum[p] + value
    result = []
    for i in range(4):
        for j in range(4):
            p = 4 * i + j
            edges = (i in (0, 3)) + (j in (0, 3))
            total = slabs[p] * float(stiff[i, i] + stiff[j, j] - PENALTY * edges)
            for q in range(4):
                if q != i:
                    total = total + slabs[4 * q + j] * float(stiff[i, q])
                if q != j:
                    total = total + slabs[4 * i + q] * float(stiff[j, q])
            if edges:
                total = total + PENALTY * edge_sum[p]
            result.append(metric * total)
    return result


def turned_of(table_ref):
    return [jnp.broadcast_to(table_ref[s : s + 1, :], (8, ELEM)) == 1 for s in range(4, 8)]


def first_kernel(
    tracer_ref, metric_ref, table_ref, below_ref, above_ref, west_ref, east_ref,
    first_ref, row_ref, col_ref, edges, across,
):
    fill_edges(edges, lambda p: tracer_ref[pl.ds(p, LEV, stride=PTS), :])
    gather_across(edges, across, table_ref, (below_ref, above_ref, west_ref, east_ref))
    metric = metric_ref[...]

    def block(b, carry):
        at = pl.ds(pl.multiple_of(b * 8, 8), 8)
        slabs = [tracer_ref[pl.ds(b * (8 * PTS) + p, 8, stride=PTS), :] for p in range(PTS)]
        result = operator(slabs, metric, turned_of(table_ref), across, b)
        for p in range(PTS):
            first_ref[p, at, :] = result[p]
        return carry

    lax.fori_loop(0, BLOCKS, block, 0)
    fill_edges(edges, lambda p: first_ref[p])
    emit(edges, table_ref[8:9, :], row_ref, col_ref)


EDGE_SCRATCH = [
    pltpu.VMEM((4 * LEV, TABLE), jnp.float32),
    pltpu.VMEM((4 * LEV, 4 * ELEM), jnp.float32),
]


def first_pass(tracer, metric, table, incoming):
    return pl.pallas_call(
        first_kernel,
        out_shape=(pltpu.VMEM((PTS, LEV, ELEM), jnp.float32), FLAT, FLAT),
        in_specs=[VMEM] * 7,
        out_specs=(VMEM, VMEM, VMEM),
        scratch_shapes=EDGE_SCRATCH,
        compiler_params=PARAMS,
        cost_estimate=cost(2.4),
        name="first_pass",
    )(*[inside(x) for x in (tracer, metric, table, *incoming)])


def second_kernel(
    tracer_ref, field_ref, metric_ref, table_ref, below_ref, above_ref, west_ref, east_ref,
    stepped_ref, edges, across,
):
    fill_edges(edges, lambda p: field_ref[p])
    gather_across(edges, across, table_ref, (below_ref, above_ref, west_ref, east_ref))
    metric = metric_ref[...]

    def block(b, carry):
        at = pl.ds(pl.multiple_of(b * 8, 8), 8)
        slabs = [field_ref[p, at, :] for p in range(PTS)]
        result = operator(slabs, metric, turned_of(table_ref), across, b)
        for p in range(PTS):
            point = pl.ds(b * (8 * PTS) + p, 8, stride=PTS)
            stepped_ref[point, :] = tracer_ref[point, :] - HYPER * result[p]
        return carry

    lax.fori_loop(0, BLOCKS, block, 0)


def second_pass(tracer, field, metric, table, incoming):
    return pl.pallas_call(
        second_kernel,
        out_shape=pltpu.VMEM((LEV * PTS, ELEM), jnp.float32),
        in_specs=[VMEM] * 8,
        out_specs=VMEM,
        scratch_shapes=EDGE_SCRATCH,
        compiler_params=PARAMS,
        cost_estimate=cost(1.2),
        name="second_pass",
    )(*[inside(x) for x in (tracer, field, metric, table, *incoming)])


def mix_kernel(reply_ref, bucket_ref, stepped_ref, out_ref, wide, data, mixing, gain, carried):
    first_half = iota((4, ELEM), 1) < PER
    for c in range(PTS):
        lanes = slice(c * ELEM, (c + 1) * ELEM)
        for b in range(BLOCKS):
            even, odd = reply_ref[2 * c, b], reply_ref[2 * c + 1, b]
            low = jnp.where(first_half, even, pltpu.roll(odd, PER, 1))
            high = jnp.where(first_half, pltpu.roll(even, PER, 1), odd)
            wide[8 * b : 8 * b + 8, lanes] = jnp.concatenate([low, high], axis=0)
    data[...] = parts_of(wide[...])
    for p in range(0, PTS, 2):
        index = jnp.concatenate([bucket_ref[p : p + 1, :], bucket_ref[p + 1 : p + 2, :]], axis=1)
        value = moved(data[...], one_hot(index, COLS))
        for u in range(2):
            mixing[pl.ds(p + u, LEV, stride=PTS), :] = value[:, u * ELEM : (u + 1) * ELEM]

    def level(ref, k):
        return ref[k * PTS : (k + 1) * PTS, :]

    zero = jnp.zeros((PTS, ELEM), jnp.float32)
    half = LEV // 2
    up_gain, up_rhs, down_gain, down_rhs = zero, zero, zero, zero
    for i in range(half):
        k = i
        here, after = level(mixing, k), level(mixing, k + 1)
        scale = 1.0 / (1.0 + after + here * (1.0 - up_gain))
        up_rhs = (level(stepped_ref, k) + here * up_rhs) * scale
        up_gain = after * scale
        if i < half - 1:
            gain[k * PTS : (k + 1) * PTS, :] = up_gain
            carried[k * PTS : (k + 1) * PTS, :] = up_rhs
        m = LEV - 1 - i
        here = level(mixing, m)
        after = zero if i == 0 else level(mixing, m + 1)
        scale = 1.0 / (1.0 + here + after * (1.0 - down_gain))
        down_rhs = (level(stepped_ref, m) + after * down_rhs) * scale
        down_gain = here * scale
        if i < half - 1:
            gain[m * PTS : (m + 1) * PTS, :] = down_gain
            carried[m * PTS : (m + 1) * PTS, :] = down_rhs
    upper = (up_rhs + up_gain * down_rhs) / (1.0 - up_gain * down_gain)
    lower = down_rhs + down_gain * upper
    out_ref[half - 1] = upper
    out_ref[half] = lower
    for i in range(half - 2, -1, -1):
        upper = level(carried, i) + level(gain, i) * upper
        out_ref[i] = upper
        m = LEV - 1 - i
        lower = level(carried, m) + level(gain, m) * lower
        out_ref[m] = lower


def mix(replied, bucket, stepped):
    rows = LEV * PTS
    return pl.pallas_call(
        mix_kernel,
        out_shape=jax.ShapeDtypeStruct((LEV, PTS, ELEM), jnp.float32),
        in_specs=[VMEM] * 3,
        out_specs=VMEM,
        scratch_shapes=[
            pltpu.VMEM((LEV, COLS), jnp.float32),
            pltpu.VMEM((2 * LEV, COLS), jnp.bfloat16),
            pltpu.VMEM((rows, ELEM), jnp.float32),
            pltpu.VMEM((rows, ELEM), jnp.float32),
            pltpu.VMEM((rows, ELEM), jnp.float32),
        ],
        compiler_params=PARAMS,
        cost_estimate=cost(2.8),
        name="mix",
    )(inside(replied), inside(bucket), inside(stepped))


def exchange(row_out, col_out):
    def both(value, axis):
        size = lax.axis_size(axis)
        up = [(i, (i + 1) % size) for i in range(size)]
        down = [(j, i) for i, j in up]
        return lax.ppermute(value, axis, up), lax.ppermute(value, axis, down)

    return both(row_out, "grp") + both(col_out, "dev")


def on_device(tracer, metric, coef, nbr_slot, edge_flip, send_slot, span_slot):
    flat = tracer.reshape(LEV * PTS, ELEM)
    asked, bucket, table, metric = route(span_slot, nbr_slot, edge_flip, send_slot, metric)
    row_out, col_out = halo(flat, table)
    got = lax.all_to_all(asked, "dev", split_axis=0, concat_axis=0, tiled=True)
    incoming = exchange(row_out, col_out)
    replied = lax.all_to_all(reply(coef, got), "dev", split_axis=0, concat_axis=0, tiled=True)
    first, row_out, col_out = first_pass(flat, metric, table, incoming)
    stepped = second_pass(flat, first, metric, table, exchange(row_out, col_out))
    return mix(replied, bucket, stepped)


def solution(mesh):
    in_specs = (
        P(None, None, ("grp", "dev")),
        P(("grp", "dev")),
        P(None, ("grp", "dev")),
        P(None, ("grp", "dev")),
        P(None, ("grp", "dev")),
        P(("grp", "dev")),
        P(None, ("grp", "dev")),
    )
    out_specs = P(None, None, ("grp", "dev"))
    return jax.shard_map(
        on_device, mesh=mesh, in_specs=in_specs, out_specs=out_specs, check_vma=False
    )
```

```python
import jax
import jax.numpy as jnp
import numpy as np
from jax import lax
from jax.experimental import pallas as pl
from jax.experimental.pallas import tpu as pltpu
from jax.sharding import PartitionSpec as P

BR = 8
BC = 16
LEV = 72
PTS = 16
ELEM = 128
COLS = PTS * ELEM
PEERS = 32
PER = COLS // PEERS
BLOCKS = LEV // 8
SCALE = 5

PENALTY = 10.0
HYPER = 0.0001

VMEM = pl.BlockSpec(memory_space=pltpu.VMEM)
PARAMS = pltpu.CompilerParams(vmem_limit_bytes=8 << 20)

EDGE_POINT = [[0, 1, 2, 3], [3, 7, 11, 15], [12, 13, 14, 15], [0, 4, 8, 12]]


def stiffness():
    nodes = np.array([-1.0, -1.0 / np.sqrt(5.0), 1.0 / np.sqrt(5.0), 1.0])
    weights = np.array([1.0 / 6.0, 5.0 / 6.0, 5.0 / 6.0, 1.0 / 6.0])
    lambdas = np.ones(4)
    for j in range(4):
        for k in range(4):
            if k != j:
                lambdas[j] = lambdas[j] / (nodes[j] - nodes[k])
    deriv = np.zeros((4, 4))
    for i in range(4):
        for j in range(4):
            if i != j:
                deriv[i, j] = lambdas[j] / lambdas[i] / (nodes[i] - nodes[j])
        deriv[i, i] = -np.sum(deriv[i])
    return -(deriv.T * weights[None, :] @ deriv) / weights[:, None]


def iota(shape, dim):
    return lax.broadcasted_iota(jnp.int32, shape, dim)


def outside(value):
    return pltpu.with_memory_space_constraint(value, pltpu.HBM)


def parts_of(value):
    high = value.astype(jnp.bfloat16)
    low = (value - high.astype(jnp.float32)).astype(jnp.bfloat16)
    return jnp.concatenate([high, low], axis=0)


def moved(stacked, hot):
    product = jnp.dot(stacked, hot, preferred_element_type=jnp.float32)
    half = product.shape[0] // 2
    return product[:half] + product[half:]


def one_hot(index, depth):
    width = index.shape[1]
    low, high = index & (ELEM - 1), index >> 7
    base = jnp.broadcast_to(low, (ELEM, width)) == iota((ELEM, width), 0)
    base = jnp.where(base, 1.0, 0.0).astype(jnp.bfloat16)
    return jnp.concatenate(
        [
            base * jnp.broadcast_to(jnp.where(high == h, 1.0, 0.0), (ELEM, width)).astype(jnp.bfloat16)
            for h in range(depth // ELEM)
        ],
        axis=0,
    )


def cost(micros):
    work = int(SCALE * micros * 1e9)
    return pl.CostEstimate(flops=work, bytes_accessed=1 << 20, transcendentals=0)


def inside(value):
    return pltpu.with_memory_space_constraint(value, pltpu.VMEM)


def route_kernel(
    span_ref, nbr_ref, flip_ref, send_ref, metric_ref, req_ref, bucket_ref, table_ref, scale_ref
):
    table_ref[0:4, :] = nbr_ref[...]
    table_ref[4:8, :] = flip_ref[...]
    table_ref[8:16, :] = jnp.full((8, ELEM), 4 * ELEM, jnp.int32)
    table_ref[8:9, : 2 * BC + 2 * BR] = send_ref[...]
    scale_ref[...] = jnp.broadcast_to(metric_ref[...], (8, ELEM))
    span = span_ref[...]
    target = span >> 11
    pos = span & (COLS - 1)
    peer = iota((PEERS, ELEM), 0)
    hot = [
        jnp.where(jnp.broadcast_to(target[p : p + 1], (PEERS, ELEM)) == peer, 1.0, 0.0)
        for p in range(PTS)
    ]
    stacked = jnp.concatenate(hot, axis=0).astype(jnp.bfloat16)
    row, col = iota((ELEM, 2 * ELEM), 0), iota((ELEM, 2 * ELEM), 1)
    ahead = jnp.where((row < col) | (col >= ELEM), 1.0, 0.0).astype(jnp.bfloat16)
    counts = jnp.dot(stacked, ahead, preferred_element_type=jnp.float32)
    base = jnp.zeros((PEERS, ELEM), jnp.float32)
    arrivals = []
    for p in range(PTS):
        here = counts[p * PEERS : (p + 1) * PEERS]
        arrivals.append(jnp.sum(hot[p] * (here[:, :ELEM] + base), axis=0, keepdims=True))
        base = base + here[:, ELEM:]
    arrival = jnp.concatenate(arrivals, axis=0).astype(jnp.int32)
    bucket_ref[...] = target * PER + arrival
    high = (pos >> 8).astype(jnp.float32)
    low = (pos & 255).astype(jnp.float32)
    slot = iota((PER, ELEM), 0)
    left, right = [], []
    for p in range(PTS):
        left.append(
            jnp.concatenate([hot[p] * high[p : p + 1], hot[p] * low[p : p + 1]], axis=0)
        )
        right.append(
            jnp.where(jnp.broadcast_to(arrival[p : p + 1], (PER, ELEM)) == slot, 1.0, 0.0)
        )
    left = jnp.concatenate(left, axis=1).astype(jnp.bfloat16)
    right = jnp.concatenate(right, axis=1).astype(jnp.bfloat16)
    right = jnp.concatenate([right, right], axis=0)
    parts = lax.dot_general(
        left, right, (((1,), (1,)), ((), ())), preferred_element_type=jnp.float32
    )
    asked = (parts[:PEERS] * 256.0 + parts[PEERS:]).astype(jnp.int32)
    for r in range(PEERS):
        req_ref[r] = asked[r : r + 1]


def reply_kernel(coef_ref, got_ref, out_ref, data):
    data[...] = parts_of(coef_ref[...])
    lane = iota((1, ELEM), 1)
    first_half = iota((8, ELEM), 1) < PER
    for pair in range(PTS // 2):
        chunks = (2 * pair, 2 * pair + 1)
        asked = [jnp.where(lane < PER, got_ref[2 * c], got_ref[2 * c + 1]) for c in chunks]
        value = moved(data[...], one_hot(jnp.concatenate(asked, axis=1), COLS))
        for u, c in enumerate(chunks):
            acc = [value[8 * b : 8 * b + 8, u * ELEM : (u + 1) * ELEM] for b in range(BLOCKS)]
            for b in range(BLOCKS):
                turned = pltpu.roll(acc[b], PER, 1)
                even = jnp.where(first_half, acc[b], pltpu.roll(turned, 4, 0))
                odd = jnp.where(first_half, turned, pltpu.roll(acc[b], 4, 0))
                out_ref[2 * c, b] = even[:4]
                out_ref[2 * c + 1, b] = odd[:4]


def reply(coef, got):
    return pl.pallas_call(
        reply_kernel,
        out_shape=pltpu.VMEM((PEERS, BLOCKS, 4, ELEM), jnp.float32),
        in_specs=[VMEM, VMEM],
        out_specs=VMEM,
        scratch_shapes=[pltpu.VMEM((2 * LEV, COLS), jnp.bfloat16)],
        compiler_params=PARAMS,
        cost_estimate=cost(2.4),
        name="reply",
    )(inside(coef), inside(got))


TABLE = 5 * ELEM


def fill_edges(edges, point):
    for t in range(4):
        for s in range(4):
            edges[t * LEV : (t + 1) * LEV, s * ELEM : (s + 1) * ELEM] = point(EDGE_POINT[s][t])


def turn(value, lanes):
    lanes = lanes % ELEM
    return pltpu.roll(value, lanes, 1) if lanes else value


def emit(edges, chosen, row_ref, east_ref, west_ref):
    out = moved(parts_of(edges[:, : 4 * ELEM]), one_hot(chosen, 4 * ELEM))
    out = [out[t * LEV : (t + 1) * LEV] for t in range(4)]
    lane = iota((LEV, ELEM), 1)
    value = out[0]
    for t in range(1, 4):
        value = jnp.where((lane >> 5) == t, turn(out[t], 32 * t), value)
    row_ref[...] = value
    lane24 = iota((THIRD, ELEM), 1)
    for start, ref in ((2 * BC, east_ref), (2 * BC + BR, west_ref)):
        value = turn(out[0], -start)
        for t in range(1, 4):
            value = jnp.where((lane >> 3) == t, turn(out[t], 8 * t - start), value)
        packed = value[:THIRD]
        for j in range(1, 3):
            block = turn(value[j * THIRD : (j + 1) * THIRD], 32 * j)
            packed = jnp.where((lane24 >> 5) == j, block, packed)
        ref[...] = packed


THIRD = LEV // 3
FLAT = pltpu.VMEM((LEV, ELEM), jnp.float32)
SIDE = pltpu.VMEM((THIRD, ELEM), jnp.float32)


def route(span_slot, nbr_slot, edge_flip, send_slot, metric):
    return pl.pallas_call(
        route_kernel,
        out_shape=(
            pltpu.VMEM((PEERS, 1, ELEM), jnp.int32),
            pltpu.VMEM((PTS, ELEM), jnp.int32),
            pltpu.VMEM((16, ELEM), jnp.int32),
            pltpu.VMEM((8, ELEM), jnp.float32),
        ),
        in_specs=[VMEM] * 5,
        out_specs=(VMEM,) * 4,
        compiler_params=PARAMS,
        cost_estimate=cost(1.2),
        name="route",
    )(*[outside(x) for x in (span_slot, nbr_slot, edge_flip, send_slot.reshape(1, -1), metric.reshape(1, ELEM))])


def halo_kernel(tracer_ref, table_ref, row_ref, east_ref, west_ref, edges):
    fill_edges(edges, lambda p: tracer_ref[pl.ds(p, LEV, stride=PTS), :])
    emit(edges, table_ref[8:9, :], row_ref, east_ref, west_ref)


def halo(tracer, table):
    return pl.pallas_call(
        halo_kernel,
        out_shape=(FLAT, SIDE, SIDE),
        in_specs=[VMEM, VMEM],
        out_specs=(VMEM,) * 3,
        scratch_shapes=[pltpu.VMEM((4 * LEV, 4 * ELEM), jnp.float32)],
        compiler_params=PARAMS,
        cost_estimate=cost(1.0),
        name="halo",
    )(inside(tracer), inside(table))


def received(incoming):
    below, above, west, east = [ref[...] for ref in incoming]
    lane = iota((LEV, ELEM), 1)
    lane24 = iota((THIRD, ELEM), 1)
    row_in = jnp.where((lane & 31) < BC, below, above)
    result = []
    for t in range(4):
        sides = [
            jnp.where(
                lane24 < 2 * BC + BR,
                turn(west, 2 * BC - (32 * j + 8 * t)),
                turn(east, 2 * BC + BR - (32 * j + 8 * t)),
            )
            for j in range(3)
        ]
        sides = jnp.concatenate(sides, axis=0)
        result.append(jnp.where(lane < 2 * BC, turn(row_in, -32 * t), sides))
    return result


def neighbours(table_ref):
    return jnp.concatenate([table_ref[s : s + 1, :] for s in range(4)], axis=1)


def edge_sums(across, turned, b):
    sums = [None] * PTS
    for s in range(4):
        raw = [
            across[pl.ds(pl.multiple_of(t * LEV + b * 8, 8), 8), s * ELEM : (s + 1) * ELEM]
            for t in range(4)
        ]
        for t in range(4):
            p = EDGE_POINT[s][t]
            value = jnp.where(turned[s], raw[3 - t], raw[t])
            sums[p] = value if sums[p] is None else sums[p] + value
    return sums


def operator(slabs, metric, turned, across, b):
    stiff = stiffness()
    edge_sum = edge_sums(across, turned, b)
    result = []
    for i in range(4):
        for j in range(4):
            p = 4 * i + j
            edges = (i in (0, 3)) + (j in (0, 3))
            total = slabs[p] * float(stiff[i, i] + stiff[j, j] - PENALTY * edges)
            for q in range(4):
                if q != i:
                    total = total + slabs[4 * q + j] * float(stiff[i, q])
                if q != j:
                    total = total + slabs[4 * i + q] * float(stiff[j, q])
            if edges:
                total = total + PENALTY * edge_sum[p]
            result.append(metric * total)
    return result


def turned_of(table_ref):
    return [jnp.broadcast_to(table_ref[s : s + 1, :], (8, ELEM)) == 1 for s in range(4, 8)]


def first_kernel(
    tracer_ref, metric_ref, table_ref, below_ref, above_ref, west_ref, east_ref,
    first_ref, row_ref, east_out, west_out, edges, across,
):
    fill_edges(edges, lambda p: tracer_ref[pl.ds(p, LEV, stride=PTS), :])
    halo_in = received((below_ref, above_ref, west_ref, east_ref))
    for t in range(4):
        edges[t * LEV : (t + 1) * LEV, 4 * ELEM :] = halo_in[t]
    across[...] = moved(parts_of(edges[...]), one_hot(neighbours(table_ref), TABLE))
    metric = metric_ref[...]

    def block(b, carry):
        at = pl.ds(pl.multiple_of(b * 8, 8), 8)
        slabs = [tracer_ref[pl.ds(b * (8 * PTS) + p, 8, stride=PTS), :] for p in range(PTS)]
        result = operator(slabs, metric, turned_of(table_ref), across, b)
        for p in range(PTS):
            first_ref[p, at, :] = result[p]
        return carry

    lax.fori_loop(0, BLOCKS, block, 0)
    fill_edges(edges, lambda p: first_ref[p])
    emit(edges, table_ref[8:9, :], row_ref, east_out, west_out)


EDGE_SCRATCH = [
    pltpu.VMEM((4 * LEV, TABLE), jnp.float32),
    pltpu.VMEM((4 * LEV, 4 * ELEM), jnp.float32),
]


def first_pass(tracer, metric, table, incoming):
    return pl.pallas_call(
        first_kernel,
        out_shape=(pltpu.VMEM((PTS, LEV, ELEM), jnp.float32), FLAT, SIDE, SIDE),
        in_specs=[VMEM] * 7,
        out_specs=(VMEM,) * 4,
        scratch_shapes=EDGE_SCRATCH,
        compiler_params=PARAMS,
        cost_estimate=cost(2.4),
        name="first_pass",
    )(*[inside(x) for x in (tracer, metric, table, *incoming)])


def second_kernel(tracer_ref, field_ref, metric_ref, table_ref, stepped_ref, edges, across):
    fill_edges(edges, lambda p: field_ref[p])
    across[...] = moved(parts_of(edges[...]), one_hot(neighbours(table_ref), 4 * ELEM))
    metric = metric_ref[...]

    def block(b, carry):
        at = pl.ds(pl.multiple_of(b * 8, 8), 8)
        slabs = [field_ref[p, at, :] for p in range(PTS)]
        result = operator(slabs, metric, turned_of(table_ref), across, b)
        for p in range(PTS):
            point = pl.ds(b * (8 * PTS) + p, 8, stride=PTS)
            stepped_ref[point, :] = tracer_ref[point, :] - HYPER * result[p]
        return carry

    lax.fori_loop(0, BLOCKS, block, 0)


def second_pass(tracer, field, metric, table):
    return pl.pallas_call(
        second_kernel,
        out_shape=pltpu.VMEM((LEV * PTS, ELEM), jnp.float32),
        in_specs=[VMEM] * 4,
        out_specs=VMEM,
        scratch_shapes=[pltpu.VMEM((4 * LEV, 4 * ELEM), jnp.float32)] * 2,
        compiler_params=PARAMS,
        cost_estimate=cost(1.2),
        name="second_pass",
    )(*[inside(x) for x in (tracer, field, metric, table)])


def finish_kernel(
    partial_ref, metric_ref, table_ref, below_ref, above_ref, west_ref, east_ref, stepped_ref, across
):
    halo_in = jnp.concatenate(received((below_ref, above_ref, west_ref, east_ref)), axis=0)
    across[...] = moved(parts_of(halo_in), one_hot(neighbours(table_ref) - 4 * ELEM, ELEM))
    weight = (HYPER * PENALTY) * metric_ref[...]

    def block(b, carry):
        sums = edge_sums(across, turned_of(table_ref), b)
        for p in range(PTS):
            point = pl.ds(b * (8 * PTS) + p, 8, stride=PTS)
            value = partial_ref[point, :]
            stepped_ref[point, :] = value if sums[p] is None else value - weight * sums[p]
        return carry

    lax.fori_loop(0, BLOCKS, block, 0)


def finish(partial, metric, table, incoming):
    return pl.pallas_call(
        finish_kernel,
        out_shape=pltpu.VMEM((LEV * PTS, ELEM), jnp.float32),
        in_specs=[VMEM] * 7,
        out_specs=VMEM,
        scratch_shapes=[pltpu.VMEM((4 * LEV, 4 * ELEM), jnp.float32)],
        compiler_params=PARAMS,
        cost_estimate=cost(0.7),
        name="finish",
    )(*[inside(x) for x in (partial, metric, table, *incoming)])


def mix_kernel(reply_ref, bucket_ref, stepped_ref, out_ref, wide, data, mixing, gain, carried):
    first_half = iota((4, ELEM), 1) < PER
    for c in range(PTS):
        lanes = slice(c * ELEM, (c + 1) * ELEM)
        for b in range(BLOCKS):
            even, odd = reply_ref[2 * c, b], reply_ref[2 * c + 1, b]
            low = jnp.where(first_half, even, pltpu.roll(odd, PER, 1))
            high = jnp.where(first_half, pltpu.roll(even, PER, 1), odd)
            wide[8 * b : 8 * b + 8, lanes] = jnp.concatenate([low, high], axis=0)
    data[...] = parts_of(wide[...])
    for p in range(0, PTS, 2):
        index = jnp.concatenate([bucket_ref[p : p + 1, :], bucket_ref[p + 1 : p + 2, :]], axis=1)
        value = moved(data[...], one_hot(index, COLS))
        for u in range(2):
            mixing[pl.ds(p + u, LEV, stride=PTS), :] = value[:, u * ELEM : (u + 1) * ELEM]

    def level(ref, k):
        return ref[k * PTS : (k + 1) * PTS, :]

    zero = jnp.zeros((PTS, ELEM), jnp.float32)
    half = LEV // 2
    up_gain, up_rhs, down_gain, down_rhs = zero, zero, zero, zero
    for i in range(half):
        k = i
        here, after = level(mixing, k), level(mixing, k + 1)
        scale = 1.0 / (1.0 + after + here * (1.0 - up_gain))
        up_rhs = (level(stepped_ref, k) + here * up_rhs) * scale
        up_gain = after * scale
        if i < half - 1:
            gain[k * PTS : (k + 1) * PTS, :] = up_gain
            carried[k * PTS : (k + 1) * PTS, :] = up_rhs
        m = LEV - 1 - i
        here = level(mixing, m)
        after = zero if i == 0 else level(mixing, m + 1)
        scale = 1.0 / (1.0 + here + after * (1.0 - down_gain))
        down_rhs = (level(stepped_ref, m) + after * down_rhs) * scale
        down_gain = here * scale
        if i < half - 1:
            gain[m * PTS : (m + 1) * PTS, :] = down_gain
            carried[m * PTS : (m + 1) * PTS, :] = down_rhs
    upper = (up_rhs + up_gain * down_rhs) / (1.0 - up_gain * down_gain)
    lower = down_rhs + down_gain * upper
    out_ref[half - 1] = upper
    out_ref[half] = lower
    for i in range(half - 2, -1, -1):
        upper = level(carried, i) + level(gain, i) * upper
        out_ref[i] = upper
        m = LEV - 1 - i
        lower = level(carried, m) + level(gain, m) * lower
        out_ref[m] = lower


def mix(replied, bucket, stepped):
    rows = LEV * PTS
    return pl.pallas_call(
        mix_kernel,
        out_shape=jax.ShapeDtypeStruct((LEV, PTS, ELEM), jnp.float32),
        in_specs=[VMEM] * 3,
        out_specs=VMEM,
        scratch_shapes=[
            pltpu.VMEM((LEV, COLS), jnp.float32),
            pltpu.VMEM((2 * LEV, COLS), jnp.bfloat16),
            pltpu.VMEM((rows, ELEM), jnp.float32),
            pltpu.VMEM((rows, ELEM), jnp.float32),
            pltpu.VMEM((rows, ELEM), jnp.float32),
        ],
        compiler_params=PARAMS,
        cost_estimate=cost(2.8),
        name="mix",
    )(*[inside(x) for x in (replied, bucket, stepped)])


def exchange(row_out, east_out, west_out):
    def moved_by(value, axis, step):
        size = lax.axis_size(axis)
        return lax.ppermute(value, axis, [(i, (i + step) % size) for i in range(size)])

    return (
        moved_by(row_out, "grp", 1),
        moved_by(row_out, "grp", -1),
        moved_by(east_out, "dev", 1),
        moved_by(west_out, "dev", -1),
    )


def on_device(tracer, metric, coef, nbr_slot, edge_flip, send_slot, span_slot):
    flat = tracer.reshape(LEV * PTS, ELEM)
    asked, bucket, table, metric = route(span_slot, nbr_slot, edge_flip, send_slot, metric)
    outgoing = halo(flat, table)
    got = lax.all_to_all(asked, "dev", split_axis=0, concat_axis=0, tiled=True)
    incoming = exchange(*outgoing)
    replied = lax.all_to_all(reply(coef, got), "dev", split_axis=0, concat_axis=0, tiled=True)
    first, *outgoing = first_pass(flat, metric, table, incoming)
    partial = second_pass(flat, first, metric, table)
    stepped = finish(partial, metric, table, exchange(*outgoing))
    return mix(replied, bucket, stepped)


def solution(mesh):
    in_specs = (
        P(None, None, ("grp", "dev")),
        P(("grp", "dev")),
        P(None, ("grp", "dev")),
        P(None, ("grp", "dev")),
        P(None, ("grp", "dev")),
        P(("grp", "dev")),
        P(None, ("grp", "dev")),
    )
    out_specs = P(None, None, ("grp", "dev"))
    return jax.shard_map(
        on_device, mesh=mesh, in_specs=in_specs, out_specs=out_specs, check_vma=False
    )
```

```python
import jax
import jax.numpy as jnp
import numpy as np
from jax import lax
from jax.experimental import pallas as pl
from jax.experimental.pallas import tpu as pltpu
from jax.sharding import PartitionSpec as P

BR = 8
BC = 16
LEV = 72
PTS = 16
ELEM = 128
COLS = PTS * ELEM
PEERS = 32
PER = COLS // PEERS
BLOCKS = LEV // 8
SCALE = 5

PENALTY = 10.0
HYPER = 0.0001

VMEM = pl.BlockSpec(memory_space=pltpu.VMEM)
PARAMS = pltpu.CompilerParams(vmem_limit_bytes=8 << 20)

EDGE_POINT = [[0, 1, 2, 3], [3, 7, 11, 15], [12, 13, 14, 15], [0, 4, 8, 12]]


def stiffness():
    nodes = np.array([-1.0, -1.0 / np.sqrt(5.0), 1.0 / np.sqrt(5.0), 1.0])
    weights = np.array([1.0 / 6.0, 5.0 / 6.0, 5.0 / 6.0, 1.0 / 6.0])
    lambdas = np.ones(4)
    for j in range(4):
        for k in range(4):
            if k != j:
                lambdas[j] = lambdas[j] / (nodes[j] - nodes[k])
    deriv = np.zeros((4, 4))
    for i in range(4):
        for j in range(4):
            if i != j:
                deriv[i, j] = lambdas[j] / lambdas[i] / (nodes[i] - nodes[j])
        deriv[i, i] = -np.sum(deriv[i])
    return -(deriv.T * weights[None, :] @ deriv) / weights[:, None]


def iota(shape, dim):
    return lax.broadcasted_iota(jnp.int32, shape, dim)


def outside(value):
    return pltpu.with_memory_space_constraint(value, pltpu.HBM)


def parts_of(value):
    high = value.astype(jnp.bfloat16)
    low = (value - high.astype(jnp.float32)).astype(jnp.bfloat16)
    return jnp.concatenate([high, low], axis=0)


def moved(stacked, hot):
    product = jnp.dot(stacked, hot, preferred_element_type=jnp.float32)
    half = product.shape[0] // 2
    return product[:half] + product[half:]


def one_hot(index, depth):
    width = index.shape[1]
    low, high = index & (ELEM - 1), index >> 7
    base = jnp.broadcast_to(low, (ELEM, width)) == iota((ELEM, width), 0)
    base = jnp.where(base, 1.0, 0.0).astype(jnp.bfloat16)
    return jnp.concatenate(
        [
            base * jnp.broadcast_to(jnp.where(high == h, 1.0, 0.0), (ELEM, width)).astype(jnp.bfloat16)
            for h in range(depth // ELEM)
        ],
        axis=0,
    )


def cost(micros):
    work = int(SCALE * micros * 1e9)
    return pl.CostEstimate(flops=work, bytes_accessed=1 << 20, transcendentals=0)


def inside(value):
    return pltpu.with_memory_space_constraint(value, pltpu.VMEM)


def route_kernel(
    span_ref, nbr_ref, flip_ref, send_ref, metric_ref, req_ref, bucket_ref, table_ref, scale_ref
):
    table_ref[0:4, :] = nbr_ref[...]
    table_ref[4:8, :] = flip_ref[...]
    table_ref[8:16, :] = jnp.full((8, ELEM), 4 * ELEM, jnp.int32)
    table_ref[8:9, : 2 * BC + 2 * BR] = send_ref[...]
    scale_ref[...] = jnp.broadcast_to(metric_ref[...], (8, ELEM))
    span = span_ref[...]
    target = span >> 11
    pos = span & (COLS - 1)
    peer = iota((PEERS, ELEM), 0)
    hot = [
        jnp.where(jnp.broadcast_to(target[p : p + 1], (PEERS, ELEM)) == peer, 1.0, 0.0)
        for p in range(PTS)
    ]
    stacked = jnp.concatenate(hot, axis=0).astype(jnp.bfloat16)
    row, col = iota((ELEM, 2 * ELEM), 0), iota((ELEM, 2 * ELEM), 1)
    ahead = jnp.where((row < col) | (col >= ELEM), 1.0, 0.0).astype(jnp.bfloat16)
    counts = jnp.dot(stacked, ahead, preferred_element_type=jnp.float32)
    base = jnp.zeros((PEERS, ELEM), jnp.float32)
    arrivals = []
    for p in range(PTS):
        here = counts[p * PEERS : (p + 1) * PEERS]
        arrivals.append(jnp.sum(hot[p] * (here[:, :ELEM] + base), axis=0, keepdims=True))
        base = base + here[:, ELEM:]
    arrival = jnp.concatenate(arrivals, axis=0).astype(jnp.int32)
    bucket_ref[...] = target * PER + arrival
    high = (pos >> 8).astype(jnp.float32)
    low = (pos & 255).astype(jnp.float32)
    slot = iota((PER, ELEM), 0)
    left, right = [], []
    for p in range(PTS):
        left.append(
            jnp.concatenate([hot[p] * high[p : p + 1], hot[p] * low[p : p + 1]], axis=0)
        )
        right.append(
            jnp.where(jnp.broadcast_to(arrival[p : p + 1], (PER, ELEM)) == slot, 1.0, 0.0)
        )
    left = jnp.concatenate(left, axis=1).astype(jnp.bfloat16)
    right = jnp.concatenate(right, axis=1).astype(jnp.bfloat16)
    right = jnp.concatenate([right, right], axis=0)
    parts = lax.dot_general(
        left, right, (((1,), (1,)), ((), ())), preferred_element_type=jnp.float32
    )
    asked = (parts[:PEERS] * 256.0 + parts[PEERS:]).astype(jnp.int32)
    for r in range(PEERS):
        req_ref[r] = asked[r : r + 1]


def reply_kernel(coef_ref, got_ref, out_hbm, data, out_ref, done):
    copies = []
    data[...] = parts_of(coef_ref[...])
    lane = iota((1, ELEM), 1)
    first_half = iota((8, ELEM), 1) < PER
    for pair in range(PTS // 2):
        chunks = (2 * pair, 2 * pair + 1)
        asked = [jnp.where(lane < PER, got_ref[2 * c], got_ref[2 * c + 1]) for c in chunks]
        value = moved(data[...], one_hot(jnp.concatenate(asked, axis=1), COLS))
        for u, c in enumerate(chunks):
            acc = [value[8 * b : 8 * b + 8, u * ELEM : (u + 1) * ELEM] for b in range(BLOCKS)]
            for b in range(BLOCKS):
                turned = pltpu.roll(acc[b], PER, 1)
                even = jnp.where(first_half, acc[b], pltpu.roll(turned, 4, 0))
                odd = jnp.where(first_half, turned, pltpu.roll(acc[b], 4, 0))
                out_ref[2 * c, b] = even[:4]
                out_ref[2 * c + 1, b] = odd[:4]
        if pair % 2:
            peers = pl.ds(4 * pair - 4, 8)
            copies.append(
                pltpu.make_async_copy(out_ref.at[peers], out_hbm.at[peers], done.at[pair // 2])
            )
            copies[-1].start()
    for copy in copies:
        copy.wait()


def reply(coef, got):
    return pl.pallas_call(
        reply_kernel,
        out_shape=jax.ShapeDtypeStruct((PEERS, BLOCKS, 4, ELEM), jnp.float32),
        in_specs=[VMEM, VMEM],
        out_specs=pl.BlockSpec(memory_space=pl.ANY),
        scratch_shapes=[
            pltpu.VMEM((2 * LEV, COLS), jnp.bfloat16),
            pltpu.VMEM((PEERS, BLOCKS, 4, ELEM), jnp.float32),
            pltpu.SemaphoreType.DMA((4,)),
        ],
        compiler_params=PARAMS,
        cost_estimate=cost(2.4),
        name="reply",
    )(inside(coef), inside(got))


TABLE = 5 * ELEM


def fill_edges(edges, point):
    for t in range(4):
        for s in range(4):
            edges[t * LEV : (t + 1) * LEV, s * ELEM : (s + 1) * ELEM] = point(EDGE_POINT[s][t])


def turn(value, lanes):
    lanes = lanes % ELEM
    return pltpu.roll(value, lanes, 1) if lanes else value


def emit(edges, chosen, row_ref, east_ref, west_ref):
    out = moved(parts_of(edges[:, : 4 * ELEM]), one_hot(chosen, 4 * ELEM))
    out = [out[t * LEV : (t + 1) * LEV] for t in range(4)]
    lane = iota((LEV, ELEM), 1)
    value = out[0]
    for t in range(1, 4):
        value = jnp.where((lane >> 5) == t, turn(out[t], 32 * t), value)
    row_ref[...] = value
    lane24 = iota((THIRD, ELEM), 1)
    for start, ref in ((2 * BC, east_ref), (2 * BC + BR, west_ref)):
        value = turn(out[0], -start)
        for t in range(1, 4):
            value = jnp.where((lane >> 3) == t, turn(out[t], 8 * t - start), value)
        packed = value[:THIRD]
        for j in range(1, 3):
            block = turn(value[j * THIRD : (j + 1) * THIRD], 32 * j)
            packed = jnp.where((lane24 >> 5) == j, block, packed)
        ref[...] = packed


THIRD = LEV // 3
FLAT = pltpu.VMEM((LEV, ELEM), jnp.float32)
SIDE = pltpu.VMEM((THIRD, ELEM), jnp.float32)


def route(span_slot, nbr_slot, edge_flip, send_slot, metric):
    return pl.pallas_call(
        route_kernel,
        out_shape=(
            pltpu.VMEM((PEERS, 1, ELEM), jnp.int32),
            pltpu.VMEM((PTS, ELEM), jnp.int32),
            pltpu.VMEM((16, ELEM), jnp.int32),
            pltpu.VMEM((8, ELEM), jnp.float32),
        ),
        in_specs=[VMEM] * 5,
        out_specs=(VMEM,) * 4,
        compiler_params=PARAMS,
        cost_estimate=cost(1.2),
        name="route",
    )(*[outside(x) for x in (span_slot, nbr_slot, edge_flip, send_slot.reshape(1, -1), metric.reshape(1, ELEM))])


def halo_kernel(tracer_ref, table_ref, row_ref, east_ref, west_ref, edges):
    fill_edges(edges, lambda p: tracer_ref[pl.ds(p, LEV, stride=PTS), :])
    emit(edges, table_ref[8:9, :], row_ref, east_ref, west_ref)


def halo(tracer, table):
    return pl.pallas_call(
        halo_kernel,
        out_shape=(FLAT, SIDE, SIDE),
        in_specs=[VMEM, VMEM],
        out_specs=(VMEM,) * 3,
        scratch_shapes=[pltpu.VMEM((4 * LEV, 4 * ELEM), jnp.float32)],
        compiler_params=PARAMS,
        cost_estimate=cost(1.0),
        name="halo",
    )(inside(tracer), inside(table))


def received(incoming):
    below, above, west, east = [ref[...] for ref in incoming]
    lane = iota((LEV, ELEM), 1)
    lane24 = iota((THIRD, ELEM), 1)
    row_in = jnp.where((lane & 31) < BC, below, above)
    result = []
    for t in range(4):
        sides = [
            jnp.where(
                lane24 < 2 * BC + BR,
                turn(west, 2 * BC - (32 * j + 8 * t)),
                turn(east, 2 * BC + BR - (32 * j + 8 * t)),
            )
            for j in range(3)
        ]
        sides = jnp.concatenate(sides, axis=0)
        result.append(jnp.where(lane < 2 * BC, turn(row_in, -32 * t), sides))
    return result


def neighbours(table_ref):
    return jnp.concatenate([table_ref[s : s + 1, :] for s in range(4)], axis=1)


def edge_sums(across, turned, b):
    sums = [None] * PTS
    for s in range(4):
        raw = [
            across[pl.ds(pl.multiple_of(t * LEV + b * 8, 8), 8), s * ELEM : (s + 1) * ELEM]
            for t in range(4)
        ]
        for t in range(4):
            p = EDGE_POINT[s][t]
            value = jnp.where(turned[s], raw[3 - t], raw[t])
            sums[p] = value if sums[p] is None else sums[p] + value
    return sums


def operator(slabs, metric, turned, across, b):
    stiff = stiffness()
    edge_sum = edge_sums(across, turned, b)
    result = []
    for i in range(4):
        for j in range(4):
            p = 4 * i + j
            edges = (i in (0, 3)) + (j in (0, 3))
            total = slabs[p] * float(stiff[i, i] + stiff[j, j] - PENALTY * edges)
            for q in range(4):
                if q != i:
                    total = total + slabs[4 * q + j] * float(stiff[i, q])
                if q != j:
                    total = total + slabs[4 * i + q] * float(stiff[j, q])
            if edges:
                total = total + PENALTY * edge_sum[p]
            result.append(metric * total)
    return result


def turned_of(table_ref):
    return [jnp.broadcast_to(table_ref[s : s + 1, :], (8, ELEM)) == 1 for s in range(4, 8)]


def first_kernel(
    tracer_ref, metric_ref, table_ref, below_ref, above_ref, west_ref, east_ref,
    first_ref, row_ref, east_out, west_out, edges, across,
):
    fill_edges(edges, lambda p: tracer_ref[pl.ds(p, LEV, stride=PTS), :])
    halo_in = received((below_ref, above_ref, west_ref, east_ref))
    for t in range(4):
        edges[t * LEV : (t + 1) * LEV, 4 * ELEM :] = halo_in[t]
    across[...] = moved(parts_of(edges[...]), one_hot(neighbours(table_ref), TABLE))
    metric = metric_ref[...]

    def block(b, carry):
        at = pl.ds(pl.multiple_of(b * 8, 8), 8)
        slabs = [tracer_ref[pl.ds(b * (8 * PTS) + p, 8, stride=PTS), :] for p in range(PTS)]
        result = operator(slabs, metric, turned_of(table_ref), across, b)
        for p in range(PTS):
            first_ref[p, at, :] = result[p]
        return carry

    lax.fori_loop(0, BLOCKS, block, 0, unroll=True)
    fill_edges(edges, lambda p: first_ref[p])
    emit(edges, table_ref[8:9, :], row_ref, east_out, west_out)


EDGE_SCRATCH = [
    pltpu.VMEM((4 * LEV, TABLE), jnp.float32),
    pltpu.VMEM((4 * LEV, 4 * ELEM), jnp.float32),
]


def first_pass(tracer, metric, table, incoming):
    return pl.pallas_call(
        first_kernel,
        out_shape=(pltpu.VMEM((PTS, LEV, ELEM), jnp.float32), FLAT, SIDE, SIDE),
        in_specs=[VMEM] * 7,
        out_specs=(VMEM,) * 4,
        scratch_shapes=EDGE_SCRATCH,
        compiler_params=PARAMS,
        cost_estimate=cost(2.4),
        name="first_pass",
    )(*[inside(x) for x in (tracer, metric, table, *incoming)])


def second_kernel(tracer_ref, field_ref, metric_ref, table_ref, stepped_ref, edges, across):
    fill_edges(edges, lambda p: field_ref[p])
    across[...] = moved(parts_of(edges[...]), one_hot(neighbours(table_ref), 4 * ELEM))
    metric = metric_ref[...]

    def block(b, carry):
        at = pl.ds(pl.multiple_of(b * 8, 8), 8)
        slabs = [field_ref[p, at, :] for p in range(PTS)]
        result = operator(slabs, metric, turned_of(table_ref), across, b)
        for p in range(PTS):
            point = pl.ds(b * (8 * PTS) + p, 8, stride=PTS)
            stepped_ref[point, :] = tracer_ref[point, :] - HYPER * result[p]
        return carry

    lax.fori_loop(0, BLOCKS, block, 0, unroll=True)


def second_pass(tracer, field, metric, table):
    return pl.pallas_call(
        second_kernel,
        out_shape=pltpu.VMEM((LEV * PTS, ELEM), jnp.float32),
        in_specs=[VMEM] * 4,
        out_specs=VMEM,
        scratch_shapes=[pltpu.VMEM((4 * LEV, 4 * ELEM), jnp.float32)] * 2,
        compiler_params=PARAMS,
        cost_estimate=cost(1.2),
        name="second_pass",
    )(*[inside(x) for x in (tracer, field, metric, table)])


def finish_kernel(
    partial_ref, metric_ref, table_ref, below_ref, above_ref, west_ref, east_ref, stepped_ref, across
):
    halo_in = jnp.concatenate(received((below_ref, above_ref, west_ref, east_ref)), axis=0)
    across[...] = moved(parts_of(halo_in), one_hot(neighbours(table_ref) - 4 * ELEM, ELEM))
    weight = (HYPER * PENALTY) * metric_ref[...]

    def block(b, carry):
        sums = edge_sums(across, turned_of(table_ref), b)
        for p in range(PTS):
            point = pl.ds(b * (8 * PTS) + p, 8, stride=PTS)
            value = partial_ref[point, :]
            stepped_ref[point, :] = value if sums[p] is None else value - weight * sums[p]
        return carry

    lax.fori_loop(0, BLOCKS, block, 0, unroll=True)


def finish(partial, metric, table, incoming):
    return pl.pallas_call(
        finish_kernel,
        out_shape=pltpu.VMEM((LEV * PTS, ELEM), jnp.float32),
        in_specs=[VMEM] * 7,
        out_specs=VMEM,
        scratch_shapes=[pltpu.VMEM((4 * LEV, 4 * ELEM), jnp.float32)],
        compiler_params=PARAMS,
        cost_estimate=cost(0.7),
        name="finish",
    )(*[inside(x) for x in (partial, metric, table, *incoming)])


def mix_kernel(reply_ref, bucket_ref, stepped_ref, out_ref, wide, data, mixing, gain, carried):
    first_half = iota((4, ELEM), 1) < PER
    for c in range(PTS):
        lanes = slice(c * ELEM, (c + 1) * ELEM)
        for b in range(BLOCKS):
            even, odd = reply_ref[2 * c, b], reply_ref[2 * c + 1, b]
            low = jnp.where(first_half, even, pltpu.roll(odd, PER, 1))
            high = jnp.where(first_half, pltpu.roll(even, PER, 1), odd)
            wide[8 * b : 8 * b + 8, lanes] = jnp.concatenate([low, high], axis=0)
    data[...] = parts_of(wide[...])
    for p in range(0, PTS, 2):
        index = jnp.concatenate([bucket_ref[p : p + 1, :], bucket_ref[p + 1 : p + 2, :]], axis=1)
        value = moved(data[...], one_hot(index, COLS))
        for u in range(2):
            mixing[pl.ds(p + u, LEV, stride=PTS), :] = value[:, u * ELEM : (u + 1) * ELEM]

    def level(ref, k):
        return ref[k * PTS : (k + 1) * PTS, :]

    zero = jnp.zeros((PTS, ELEM), jnp.float32)
    half = LEV // 2
    up_gain, up_rhs, down_gain, down_rhs = zero, zero, zero, zero
    for i in range(half):
        k = i
        here, after = level(mixing, k), level(mixing, k + 1)
        scale = 1.0 / (1.0 + after + here * (1.0 - up_gain))
        up_rhs = (level(stepped_ref, k) + here * up_rhs) * scale
        up_gain = after * scale
        if i < half - 1:
            gain[k * PTS : (k + 1) * PTS, :] = up_gain
            carried[k * PTS : (k + 1) * PTS, :] = up_rhs
        m = LEV - 1 - i
        here = level(mixing, m)
        after = zero if i == 0 else level(mixing, m + 1)
        scale = 1.0 / (1.0 + here + after * (1.0 - down_gain))
        down_rhs = (level(stepped_ref, m) + after * down_rhs) * scale
        down_gain = here * scale
        if i < half - 1:
            gain[m * PTS : (m + 1) * PTS, :] = down_gain
            carried[m * PTS : (m + 1) * PTS, :] = down_rhs
    upper = (up_rhs + up_gain * down_rhs) / (1.0 - up_gain * down_gain)
    lower = down_rhs + down_gain * upper
    out_ref[half - 1] = upper
    out_ref[half] = lower
    for i in range(half - 2, -1, -1):
        upper = level(carried, i) + level(gain, i) * upper
        out_ref[i] = upper
        m = LEV - 1 - i
        lower = level(carried, m) + level(gain, m) * lower
        out_ref[m] = lower


def mix(replied, bucket, stepped):
    rows = LEV * PTS
    return pl.pallas_call(
        mix_kernel,
        out_shape=jax.ShapeDtypeStruct((LEV, PTS, ELEM), jnp.float32),
        in_specs=[VMEM] * 3,
        out_specs=VMEM,
        scratch_shapes=[
            pltpu.VMEM((LEV, COLS), jnp.float32),
            pltpu.VMEM((2 * LEV, COLS), jnp.bfloat16),
            pltpu.VMEM((rows, ELEM), jnp.float32),
            pltpu.VMEM((rows, ELEM), jnp.float32),
            pltpu.VMEM((rows, ELEM), jnp.float32),
        ],
        compiler_params=PARAMS,
        cost_estimate=cost(2.8),
        name="mix",
    )(*[inside(x) for x in (replied, bucket, stepped)])


def exchange(row_out, east_out, west_out):
    def moved_by(value, axis, step):
        size = lax.axis_size(axis)
        return lax.ppermute(value, axis, [(i, (i + step) % size) for i in range(size)])

    return (
        moved_by(row_out, "grp", 1),
        moved_by(row_out, "grp", -1),
        moved_by(east_out, "dev", 1),
        moved_by(west_out, "dev", -1),
    )


def on_device(tracer, metric, coef, nbr_slot, edge_flip, send_slot, span_slot):
    flat = tracer.reshape(LEV * PTS, ELEM)
    asked, bucket, table, metric = route(span_slot, nbr_slot, edge_flip, send_slot, metric)
    outgoing = halo(flat, table)
    got = lax.all_to_all(asked, "dev", split_axis=0, concat_axis=0, tiled=True)
    incoming = exchange(*outgoing)
    replied = lax.all_to_all(reply(coef, got), "dev", split_axis=0, concat_axis=0, tiled=True)
    first, *outgoing = first_pass(flat, metric, table, incoming)
    partial = second_pass(flat, first, metric, table)
    stepped = finish(partial, metric, table, exchange(*outgoing))
    return mix(replied, bucket, stepped)


def solution(mesh):
    in_specs = (
        P(None, None, ("grp", "dev")),
        P(("grp", "dev")),
        P(None, ("grp", "dev")),
        P(None, ("grp", "dev")),
        P(None, ("grp", "dev")),
        P(("grp", "dev")),
        P(None, ("grp", "dev")),
    )
    out_specs = P(None, None, ("grp", "dev"))
    return jax.shard_map(
        on_device, mesh=mesh, in_specs=in_specs, out_specs=out_specs, check_vma=False
    )
```

```python
import jax
import jax.numpy as jnp
import numpy as np
from jax import lax
from jax.experimental import pallas as pl
from jax.experimental.pallas import tpu as pltpu
from jax.sharding import PartitionSpec as P

BR = 8
BC = 16
LEV = 72
PTS = 16
ELEM = 128
COLS = PTS * ELEM
PEERS = 32
PER = COLS // PEERS
BLOCKS = LEV // 8
SCALE = 5

PENALTY = 10.0
HYPER = 0.0001

VMEM = pl.BlockSpec(memory_space=pltpu.VMEM)
PARAMS = pltpu.CompilerParams(vmem_limit_bytes=8 << 20)

EDGE_POINT = [[0, 1, 2, 3], [3, 7, 11, 15], [12, 13, 14, 15], [0, 4, 8, 12]]


def stiffness():
    nodes = np.array([-1.0, -1.0 / np.sqrt(5.0), 1.0 / np.sqrt(5.0), 1.0])
    weights = np.array([1.0 / 6.0, 5.0 / 6.0, 5.0 / 6.0, 1.0 / 6.0])
    lambdas = np.ones(4)
    for j in range(4):
        for k in range(4):
            if k != j:
                lambdas[j] = lambdas[j] / (nodes[j] - nodes[k])
    deriv = np.zeros((4, 4))
    for i in range(4):
        for j in range(4):
            if i != j:
                deriv[i, j] = lambdas[j] / lambdas[i] / (nodes[i] - nodes[j])
        deriv[i, i] = -np.sum(deriv[i])
    return -(deriv.T * weights[None, :] @ deriv) / weights[:, None]


def iota(shape, dim):
    return lax.broadcasted_iota(jnp.int32, shape, dim)


def outside(value):
    return pltpu.with_memory_space_constraint(value, pltpu.HBM)


def parts_of(value):
    high = value.astype(jnp.bfloat16)
    low = (value - high.astype(jnp.float32)).astype(jnp.bfloat16)
    return jnp.concatenate([high, low], axis=0)


def moved(stacked, hot):
    product = jnp.dot(stacked, hot, preferred_element_type=jnp.float32)
    half = product.shape[0] // 2
    return product[:half] + product[half:]


def one_hot(index, depth):
    width = index.shape[1]
    low, high = index & (ELEM - 1), index >> 7
    base = jnp.broadcast_to(low, (ELEM, width)) == iota((ELEM, width), 0)
    base = jnp.where(base, 1.0, 0.0).astype(jnp.bfloat16)
    return jnp.concatenate(
        [
            base * jnp.broadcast_to(jnp.where(high == h, 1.0, 0.0), (ELEM, width)).astype(jnp.bfloat16)
            for h in range(depth // ELEM)
        ],
        axis=0,
    )


def cost(micros):
    work = int(SCALE * micros * 1e9)
    return pl.CostEstimate(flops=work, bytes_accessed=1 << 20, transcendentals=0)


def inside(value):
    return pltpu.with_memory_space_constraint(value, pltpu.VMEM)


def route_kernel(
    span_ref, nbr_ref, flip_ref, send_ref, metric_ref, req_ref, bucket_ref, table_ref, scale_ref
):
    table_ref[0:4, :] = nbr_ref[...]
    table_ref[4:8, :] = flip_ref[...]
    table_ref[8:16, :] = jnp.full((8, ELEM), 4 * ELEM, jnp.int32)
    table_ref[8:9, : 2 * BC + 2 * BR] = send_ref[...]
    scale_ref[...] = jnp.broadcast_to(metric_ref[...], (8, ELEM))
    span = span_ref[...]
    target = span >> 11
    pos = span & (COLS - 1)
    peer = iota((PEERS, ELEM), 0)
    hot = [
        jnp.where(jnp.broadcast_to(target[p : p + 1], (PEERS, ELEM)) == peer, 1.0, 0.0)
        for p in range(PTS)
    ]
    stacked = jnp.concatenate(hot, axis=0).astype(jnp.bfloat16)
    row, col = iota((ELEM, 2 * ELEM), 0), iota((ELEM, 2 * ELEM), 1)
    ahead = jnp.where((row < col) | (col >= ELEM), 1.0, 0.0).astype(jnp.bfloat16)
    counts = jnp.dot(stacked, ahead, preferred_element_type=jnp.float32)
    base = jnp.zeros((PEERS, ELEM), jnp.float32)
    arrivals = []
    for p in range(PTS):
        here = counts[p * PEERS : (p + 1) * PEERS]
        arrivals.append(jnp.sum(hot[p] * (here[:, :ELEM] + base), axis=0, keepdims=True))
        base = base + here[:, ELEM:]
    arrival = jnp.concatenate(arrivals, axis=0).astype(jnp.int32)
    bucket_ref[...] = target * PER + arrival
    high = (pos >> 8).astype(jnp.float32)
    low = (pos & 255).astype(jnp.float32)
    slot = iota((PER, ELEM), 0)
    left, right = [], []
    for p in range(PTS):
        left.append(
            jnp.concatenate([hot[p] * high[p : p + 1], hot[p] * low[p : p + 1]], axis=0)
        )
        right.append(
            jnp.where(jnp.broadcast_to(arrival[p : p + 1], (PER, ELEM)) == slot, 1.0, 0.0)
        )
    left = jnp.concatenate(left, axis=1).astype(jnp.bfloat16)
    right = jnp.concatenate(right, axis=1).astype(jnp.bfloat16)
    right = jnp.concatenate([right, right], axis=0)
    parts = lax.dot_general(
        left, right, (((1,), (1,)), ((), ())), preferred_element_type=jnp.float32
    )
    asked = (parts[:PEERS] * 256.0 + parts[PEERS:]).astype(jnp.int32)
    for r in range(PEERS):
        req_ref[r] = asked[r : r + 1]


def reply_kernel(coef_ref, got_ref, out_hbm, data, out_ref, done):
    copies = []
    data[...] = parts_of(coef_ref[...])
    lane = iota((1, ELEM), 1)
    first_half = iota((8, ELEM), 1) < PER
    for pair in range(PTS // 2):
        chunks = (2 * pair, 2 * pair + 1)
        asked = [jnp.where(lane < PER, got_ref[2 * c], got_ref[2 * c + 1]) for c in chunks]
        value = moved(data[...], one_hot(jnp.concatenate(asked, axis=1), COLS))
        for u, c in enumerate(chunks):
            acc = [value[8 * b : 8 * b + 8, u * ELEM : (u + 1) * ELEM] for b in range(BLOCKS)]
            for b in range(BLOCKS):
                turned = pltpu.roll(acc[b], PER, 1)
                even = jnp.where(first_half, acc[b], pltpu.roll(turned, 4, 0))
                odd = jnp.where(first_half, turned, pltpu.roll(acc[b], 4, 0))
                out_ref[2 * c, b] = even[:4]
                out_ref[2 * c + 1, b] = odd[:4]
        if pair % 2:
            peers = pl.ds(4 * pair - 4, 8)
            copies.append(
                pltpu.make_async_copy(out_ref.at[peers], out_hbm.at[peers], done.at[pair // 2])
            )
            copies[-1].start()
    for copy in copies:
        copy.wait()


def reply(coef, got):
    return pl.pallas_call(
        reply_kernel,
        out_shape=jax.ShapeDtypeStruct((PEERS, BLOCKS, 4, ELEM), jnp.float32),
        in_specs=[VMEM, VMEM],
        out_specs=pl.BlockSpec(memory_space=pl.ANY),
        scratch_shapes=[
            pltpu.VMEM((2 * LEV, COLS), jnp.bfloat16),
            pltpu.VMEM((PEERS, BLOCKS, 4, ELEM), jnp.float32),
            pltpu.SemaphoreType.DMA((4,)),
        ],
        compiler_params=PARAMS,
        cost_estimate=cost(2.4),
        name="reply",
    )(inside(coef), inside(got))


TABLE = 5 * ELEM


def fill_edges(edges, point):
    for t in range(4):
        for s in range(4):
            edges[t * LEV : (t + 1) * LEV, s * ELEM : (s + 1) * ELEM] = point(EDGE_POINT[s][t])


def turn(value, lanes):
    lanes = lanes % ELEM
    return pltpu.roll(value, lanes, 1) if lanes else value


def emit(edges, chosen, row_ref, east_ref, west_ref):
    out = moved(parts_of(edges[:, : 4 * ELEM]), one_hot(chosen, 4 * ELEM))
    out = [out[t * LEV : (t + 1) * LEV] for t in range(4)]
    lane = iota((LEV, ELEM), 1)
    value = out[0]
    for t in range(1, 4):
        value = jnp.where((lane >> 5) == t, turn(out[t], 32 * t), value)
    row_ref[...] = value
    lane24 = iota((THIRD, ELEM), 1)
    for start, ref in ((2 * BC, east_ref), (2 * BC + BR, west_ref)):
        value = turn(out[0], -start)
        for t in range(1, 4):
            value = jnp.where((lane >> 3) == t, turn(out[t], 8 * t - start), value)
        packed = value[:THIRD]
        for j in range(1, 3):
            block = turn(value[j * THIRD : (j + 1) * THIRD], 32 * j)
            packed = jnp.where((lane24 >> 5) == j, block, packed)
        ref[...] = packed


THIRD = LEV // 3
FLAT = pltpu.VMEM((LEV, ELEM), jnp.float32)
SIDE = pltpu.VMEM((THIRD, ELEM), jnp.float32)


def route(span_slot, nbr_slot, edge_flip, send_slot, metric):
    return pl.pallas_call(
        route_kernel,
        out_shape=(
            pltpu.VMEM((PEERS, 1, ELEM), jnp.int32),
            pltpu.VMEM((PTS, ELEM), jnp.int32),
            pltpu.VMEM((16, ELEM), jnp.int32),
            pltpu.VMEM((8, ELEM), jnp.float32),
        ),
        in_specs=[VMEM] * 5,
        out_specs=(VMEM,) * 4,
        compiler_params=PARAMS,
        cost_estimate=cost(1.2),
        name="route",
    )(*[outside(x) for x in (span_slot, nbr_slot, edge_flip, send_slot.reshape(1, -1), metric.reshape(1, ELEM))])


def halo_kernel(tracer_ref, table_ref, row_ref, east_ref, west_ref, edges):
    fill_edges(edges, lambda p: tracer_ref[pl.ds(p, LEV, stride=PTS), :])
    emit(edges, table_ref[8:9, :], row_ref, east_ref, west_ref)


def halo(tracer, table):
    return pl.pallas_call(
        halo_kernel,
        out_shape=(FLAT, SIDE, SIDE),
        in_specs=[VMEM, VMEM],
        out_specs=(VMEM,) * 3,
        scratch_shapes=[pltpu.VMEM((4 * LEV, 4 * ELEM), jnp.float32)],
        compiler_params=PARAMS,
        cost_estimate=cost(1.0),
        name="halo",
    )(inside(tracer), inside(table))


def received(incoming):
    below, above, west, east = [ref[...] for ref in incoming]
    lane = iota((LEV, ELEM), 1)
    lane24 = iota((THIRD, ELEM), 1)
    row_in = jnp.where((lane & 31) < BC, below, above)
    result = []
    for t in range(4):
        sides = [
            jnp.where(
                lane24 < 2 * BC + BR,
                turn(west, 2 * BC - (32 * j + 8 * t)),
                turn(east, 2 * BC + BR - (32 * j + 8 * t)),
            )
            for j in range(3)
        ]
        sides = jnp.concatenate(sides, axis=0)
        result.append(jnp.where(lane < 2 * BC, turn(row_in, -32 * t), sides))
    return result


def neighbours(table_ref):
    return jnp.concatenate([table_ref[s : s + 1, :] for s in range(4)], axis=1)


def edge_sums(across, turned, b):
    sums = [None] * PTS
    for s in range(4):
        raw = [
            across[pl.ds(pl.multiple_of(t * LEV + b * 8, 8), 8), s * ELEM : (s + 1) * ELEM]
            for t in range(4)
        ]
        for t in range(4):
            p = EDGE_POINT[s][t]
            value = jnp.where(turned[s], raw[3 - t], raw[t])
            sums[p] = value if sums[p] is None else sums[p] + value
    return sums


def operator(slabs, metric, turned, across, b):
    stiff = stiffness()
    edge_sum = edge_sums(across, turned, b)
    result = []
    for i in range(4):
        for j in range(4):
            p = 4 * i + j
            edges = (i in (0, 3)) + (j in (0, 3))
            total = slabs[p] * float(stiff[i, i] + stiff[j, j] - PENALTY * edges)
            for q in range(4):
                if q != i:
                    total = total + slabs[4 * q + j] * float(stiff[i, q])
                if q != j:
                    total = total + slabs[4 * i + q] * float(stiff[j, q])
            if edges:
                total = total + PENALTY * edge_sum[p]
            result.append(metric * total)
    return result


def turned_of(table_ref):
    return [jnp.broadcast_to(table_ref[s : s + 1, :], (8, ELEM)) == 1 for s in range(4, 8)]


def first_kernel(
    tracer_ref, metric_ref, table_ref, below_ref, above_ref, west_ref, east_ref,
    first_ref, row_ref, east_out, west_out, edges, across,
):
    fill_edges(edges, lambda p: tracer_ref[pl.ds(p, LEV, stride=PTS), :])
    halo_in = received((below_ref, above_ref, west_ref, east_ref))
    for t in range(4):
        edges[t * LEV : (t + 1) * LEV, 4 * ELEM :] = halo_in[t]
    across[...] = moved(parts_of(edges[...]), one_hot(neighbours(table_ref), TABLE))
    metric = metric_ref[...]

    def block(b, carry):
        at = pl.ds(pl.multiple_of(b * 8, 8), 8)
        slabs = [tracer_ref[pl.ds(b * (8 * PTS) + p, 8, stride=PTS), :] for p in range(PTS)]
        result = operator(slabs, metric, turned_of(table_ref), across, b)
        for p in range(PTS):
            first_ref[p, at, :] = result[p]
        return carry

    lax.fori_loop(0, BLOCKS, block, 0, unroll=True)
    fill_edges(edges, lambda p: first_ref[p])
    emit(edges, table_ref[8:9, :], row_ref, east_out, west_out)


EDGE_SCRATCH = [
    pltpu.VMEM((4 * LEV, TABLE), jnp.float32),
    pltpu.VMEM((4 * LEV, 4 * ELEM), jnp.float32),
]


def first_pass(tracer, metric, table, incoming):
    return pl.pallas_call(
        first_kernel,
        out_shape=(pltpu.VMEM((PTS, LEV, ELEM), jnp.float32), FLAT, SIDE, SIDE),
        in_specs=[VMEM] * 7,
        out_specs=(VMEM,) * 4,
        scratch_shapes=EDGE_SCRATCH,
        compiler_params=PARAMS,
        cost_estimate=cost(0.3),
        name="first_pass",
    )(*[inside(x) for x in (tracer, metric, table, *incoming)])


def second_kernel(tracer_ref, field_ref, metric_ref, table_ref, stepped_ref, edges, across):
    fill_edges(edges, lambda p: field_ref[p])
    across[...] = moved(parts_of(edges[...]), one_hot(neighbours(table_ref), 4 * ELEM))
    metric = metric_ref[...]

    def block(b, carry):
        at = pl.ds(pl.multiple_of(b * 8, 8), 8)
        slabs = [field_ref[p, at, :] for p in range(PTS)]
        result = operator(slabs, metric, turned_of(table_ref), across, b)
        for p in range(PTS):
            point = pl.ds(b * (8 * PTS) + p, 8, stride=PTS)
            stepped_ref[point, :] = tracer_ref[point, :] - HYPER * result[p]
        return carry

    lax.fori_loop(0, BLOCKS, block, 0, unroll=True)


def second_pass(tracer, field, metric, table):
    return pl.pallas_call(
        second_kernel,
        out_shape=pltpu.VMEM((LEV * PTS, ELEM), jnp.float32),
        in_specs=[VMEM] * 4,
        out_specs=VMEM,
        scratch_shapes=[pltpu.VMEM((4 * LEV, 4 * ELEM), jnp.float32)] * 2,
        compiler_params=PARAMS,
        cost_estimate=cost(0.5),
        name="second_pass",
    )(*[inside(x) for x in (tracer, field, metric, table)])


def finish_kernel(
    partial_ref, metric_ref, table_ref, below_ref, above_ref, west_ref, east_ref, stepped_ref, across
):
    halo_in = jnp.concatenate(received((below_ref, above_ref, west_ref, east_ref)), axis=0)
    across[...] = moved(parts_of(halo_in), one_hot(neighbours(table_ref) - 4 * ELEM, ELEM))
    weight = (HYPER * PENALTY) * metric_ref[...]

    def block(b, carry):
        sums = edge_sums(across, turned_of(table_ref), b)
        for p in range(PTS):
            point = pl.ds(b * (8 * PTS) + p, 8, stride=PTS)
            value = partial_ref[point, :]
            stepped_ref[point, :] = value if sums[p] is None else value - weight * sums[p]
        return carry

    lax.fori_loop(0, BLOCKS, block, 0, unroll=True)


def finish(partial, metric, table, incoming):
    return pl.pallas_call(
        finish_kernel,
        out_shape=pltpu.VMEM((LEV * PTS, ELEM), jnp.float32),
        in_specs=[VMEM] * 7,
        out_specs=VMEM,
        scratch_shapes=[pltpu.VMEM((4 * LEV, 4 * ELEM), jnp.float32)],
        compiler_params=PARAMS,
        cost_estimate=cost(0.1),
        name="finish",
    )(*[inside(x) for x in (partial, metric, table, *incoming)])


def mix_kernel(reply_ref, bucket_ref, stepped_ref, out_ref, wide, data, mixing, gain, carried):
    first_half = iota((4, ELEM), 1) < PER
    for c in range(PTS):
        lanes = slice(c * ELEM, (c + 1) * ELEM)
        for b in range(BLOCKS):
            even, odd = reply_ref[2 * c, b], reply_ref[2 * c + 1, b]
            low = jnp.where(first_half, even, pltpu.roll(odd, PER, 1))
            high = jnp.where(first_half, pltpu.roll(even, PER, 1), odd)
            wide[8 * b : 8 * b + 8, lanes] = jnp.concatenate([low, high], axis=0)
    data[...] = parts_of(wide[...])
    for p in range(0, PTS, 2):
        index = jnp.concatenate([bucket_ref[p : p + 1, :], bucket_ref[p + 1 : p + 2, :]], axis=1)
        value = moved(data[...], one_hot(index, COLS))
        for u in range(2):
            mixing[pl.ds(p + u, LEV, stride=PTS), :] = value[:, u * ELEM : (u + 1) * ELEM]

    def level(ref, k):
        return ref[k * PTS : (k + 1) * PTS, :]

    zero = jnp.zeros((PTS, ELEM), jnp.float32)
    half = LEV // 2
    up_gain, up_rhs, down_gain, down_rhs = zero, zero, zero, zero
    for i in range(half):
        k = i
        here, after = level(mixing, k), level(mixing, k + 1)
        scale = 1.0 / (1.0 + after + here * (1.0 - up_gain))
        up_rhs = (level(stepped_ref, k) + here * up_rhs) * scale
        up_gain = after * scale
        if i < half - 1:
            gain[k * PTS : (k + 1) * PTS, :] = up_gain
            carried[k * PTS : (k + 1) * PTS, :] = up_rhs
        m = LEV - 1 - i
        here = level(mixing, m)
        after = zero if i == 0 else level(mixing, m + 1)
        scale = 1.0 / (1.0 + here + after * (1.0 - down_gain))
        down_rhs = (level(stepped_ref, m) + after * down_rhs) * scale
        down_gain = here * scale
        if i < half - 1:
            gain[m * PTS : (m + 1) * PTS, :] = down_gain
            carried[m * PTS : (m + 1) * PTS, :] = down_rhs
    upper = (up_rhs + up_gain * down_rhs) / (1.0 - up_gain * down_gain)
    lower = down_rhs + down_gain * upper
    out_ref[half - 1] = upper
    out_ref[half] = lower
    for i in range(half - 2, -1, -1):
        upper = level(carried, i) + level(gain, i) * upper
        out_ref[i] = upper
        m = LEV - 1 - i
        lower = level(carried, m) + level(gain, m) * lower
        out_ref[m] = lower


def mix(replied, bucket, stepped):
    rows = LEV * PTS
    return pl.pallas_call(
        mix_kernel,
        out_shape=jax.ShapeDtypeStruct((LEV, PTS, ELEM), jnp.float32),
        in_specs=[VMEM] * 3,
        out_specs=VMEM,
        scratch_shapes=[
            pltpu.VMEM((LEV, COLS), jnp.float32),
            pltpu.VMEM((2 * LEV, COLS), jnp.bfloat16),
            pltpu.VMEM((rows, ELEM), jnp.float32),
            pltpu.VMEM((rows, ELEM), jnp.float32),
            pltpu.VMEM((rows, ELEM), jnp.float32),
        ],
        compiler_params=PARAMS,
        cost_estimate=cost(2.8),
        name="mix",
    )(*[inside(x) for x in (replied, bucket, stepped)])


def hold_kernel(value_ref, out_ref):
    out_ref[...] = value_ref[...]


def hold(value):
    return pl.pallas_call(
        hold_kernel,
        out_shape=SIDE,
        in_specs=[VMEM],
        out_specs=VMEM,
        compiler_params=PARAMS,
        cost_estimate=cost(2),
        name="hold",
    )(inside(value))


def shifted(value, axis, step):
    size = lax.axis_size(axis)
    return lax.ppermute(value, axis, [(i, (i + step) % size) for i in range(size)])


def exchange(row_out, east_out, west_out):
    return (
        shifted(row_out, "grp", 1),
        shifted(row_out, "grp", -1),
        shifted(east_out, "dev", 1),
        shifted(west_out, "dev", -1),
    )


def on_device(tracer, metric, coef, nbr_slot, edge_flip, send_slot, span_slot):
    flat = tracer.reshape(LEV * PTS, ELEM)
    asked, bucket, table, metric = route(span_slot, nbr_slot, edge_flip, send_slot, metric)
    outgoing = halo(flat, table)
    got = lax.all_to_all(asked, "dev", split_axis=0, concat_axis=0, tiled=True)
    row_out, east_out, west_out = outgoing
    sent, west_out = lax.optimization_barrier((reply(coef, got), west_out))
    incoming = exchange(row_out, east_out, hold(west_out))
    replied = lax.all_to_all(sent, "dev", split_axis=0, concat_axis=0, tiled=True)
    first, *outgoing = first_pass(flat, metric, table, incoming)
    partial = second_pass(flat, first, metric, table)
    stepped = finish(partial, metric, table, exchange(*outgoing))
    return mix(replied, bucket, stepped)


def solution(mesh):
    in_specs = (
        P(None, None, ("grp", "dev")),
        P(("grp", "dev")),
        P(None, ("grp", "dev")),
        P(None, ("grp", "dev")),
        P(None, ("grp", "dev")),
        P(("grp", "dev")),
        P(None, ("grp", "dev")),
    )
    out_specs = P(None, None, ("grp", "dev"))
    return jax.shard_map(
        on_device, mesh=mesh, in_specs=in_specs, out_specs=out_specs, check_vma=False
    )
```

```python
import jax
import jax.numpy as jnp
import numpy as np
from jax import lax
from jax.experimental import pallas as pl
from jax.experimental.pallas import tpu as pltpu
from jax.sharding import PartitionSpec as P

BR = 8
BC = 16
LEV = 72
PTS = 16
ELEM = 128
COLS = PTS * ELEM
PEERS = 32
PER = COLS // PEERS
BLOCKS = LEV // 8
SCALE = 5

PENALTY = 10.0
HYPER = 0.0001

VMEM = pl.BlockSpec(memory_space=pltpu.VMEM)
PARAMS = pltpu.CompilerParams(vmem_limit_bytes=8 << 20)

EDGE_POINT = [[0, 1, 2, 3], [3, 7, 11, 15], [12, 13, 14, 15], [0, 4, 8, 12]]


def stiffness():
    nodes = np.array([-1.0, -1.0 / np.sqrt(5.0), 1.0 / np.sqrt(5.0), 1.0])
    weights = np.array([1.0 / 6.0, 5.0 / 6.0, 5.0 / 6.0, 1.0 / 6.0])
    lambdas = np.ones(4)
    for j in range(4):
        for k in range(4):
            if k != j:
                lambdas[j] = lambdas[j] / (nodes[j] - nodes[k])
    deriv = np.zeros((4, 4))
    for i in range(4):
        for j in range(4):
            if i != j:
                deriv[i, j] = lambdas[j] / lambdas[i] / (nodes[i] - nodes[j])
        deriv[i, i] = -np.sum(deriv[i])
    return -(deriv.T * weights[None, :] @ deriv) / weights[:, None]


def iota(shape, dim):
    return lax.broadcasted_iota(jnp.int32, shape, dim)


def outside(value):
    return pltpu.with_memory_space_constraint(value, pltpu.HBM)


def parts_of(value):
    high = value.astype(jnp.bfloat16)
    low = (value - high.astype(jnp.float32)).astype(jnp.bfloat16)
    return jnp.concatenate([high, low], axis=0)


def moved(stacked, hot):
    product = jnp.dot(stacked, hot, preferred_element_type=jnp.float32)
    half = product.shape[0] // 2
    return product[:half] + product[half:]


def one_hot(index, depth):
    width = index.shape[1]
    low, high = index & (ELEM - 1), index >> 7
    base = jnp.broadcast_to(low, (ELEM, width)) == iota((ELEM, width), 0)
    base = jnp.where(base, 1.0, 0.0).astype(jnp.bfloat16)
    return jnp.concatenate(
        [
            base * jnp.broadcast_to(jnp.where(high == h, 1.0, 0.0), (ELEM, width)).astype(jnp.bfloat16)
            for h in range(depth // ELEM)
        ],
        axis=0,
    )


def cost(micros):
    work = int(SCALE * micros * 1e9)
    return pl.CostEstimate(flops=work, bytes_accessed=1 << 20, transcendentals=0)


def inside(value):
    return pltpu.with_memory_space_constraint(value, pltpu.VMEM)


def route_kernel(
    span_ref, nbr_ref, flip_ref, send_ref, metric_ref, req_ref, bucket_ref, table_ref, scale_ref
):
    table_ref[0:4, :] = nbr_ref[...]
    table_ref[4:8, :] = flip_ref[...]
    table_ref[8:16, :] = jnp.full((8, ELEM), 4 * ELEM, jnp.int32)
    table_ref[8:9, : 2 * BC + 2 * BR] = send_ref[...]
    scale_ref[...] = jnp.broadcast_to(metric_ref[...], (8, ELEM))
    span = span_ref[...]
    target = span >> 11
    pos = span & (COLS - 1)
    peer = iota((PEERS, ELEM), 0)
    hot = [
        jnp.where(jnp.broadcast_to(target[p : p + 1], (PEERS, ELEM)) == peer, 1.0, 0.0)
        for p in range(PTS)
    ]
    stacked = jnp.concatenate(hot, axis=0).astype(jnp.bfloat16)
    row, col = iota((ELEM, 2 * ELEM), 0), iota((ELEM, 2 * ELEM), 1)
    ahead = jnp.where((row < col) | (col >= ELEM), 1.0, 0.0).astype(jnp.bfloat16)
    counts = jnp.dot(stacked, ahead, preferred_element_type=jnp.float32)
    base = jnp.zeros((PEERS, ELEM), jnp.float32)
    arrivals = []
    for p in range(PTS):
        here = counts[p * PEERS : (p + 1) * PEERS]
        arrivals.append(jnp.sum(hot[p] * (here[:, :ELEM] + base), axis=0, keepdims=True))
        base = base + here[:, ELEM:]
    arrival = jnp.concatenate(arrivals, axis=0).astype(jnp.int32)
    bucket_ref[...] = target * PER + arrival
    high = (pos >> 8).astype(jnp.float32)
    low = (pos & 255).astype(jnp.float32)
    slot = iota((PER, ELEM), 0)
    left, right = [], []
    for p in range(PTS):
        left.append(
            jnp.concatenate([hot[p] * high[p : p + 1], hot[p] * low[p : p + 1]], axis=0)
        )
        right.append(
            jnp.where(jnp.broadcast_to(arrival[p : p + 1], (PER, ELEM)) == slot, 1.0, 0.0)
        )
    left = jnp.concatenate(left, axis=1).astype(jnp.bfloat16)
    right = jnp.concatenate(right, axis=1).astype(jnp.bfloat16)
    right = jnp.concatenate([right, right], axis=0)
    parts = lax.dot_general(
        left, right, (((1,), (1,)), ((), ())), preferred_element_type=jnp.float32
    )
    asked = (parts[:PEERS] * 256.0 + parts[PEERS:]).astype(jnp.int32)
    for r in range(PEERS):
        req_ref[r] = asked[r : r + 1]


def reply_kernel(coef_ref, got_ref, out_hbm, data, out_ref, done):
    copies = []
    data[...] = parts_of(coef_ref[...])
    lane = iota((1, ELEM), 1)
    first_half = iota((8, ELEM), 1) < PER
    for pair in range(PTS // 2):
        chunks = (2 * pair, 2 * pair + 1)
        asked = [jnp.where(lane < PER, got_ref[2 * c], got_ref[2 * c + 1]) for c in chunks]
        value = moved(data[...], one_hot(jnp.concatenate(asked, axis=1), COLS))
        for u, c in enumerate(chunks):
            acc = [value[8 * b : 8 * b + 8, u * ELEM : (u + 1) * ELEM] for b in range(BLOCKS)]
            for b in range(BLOCKS):
                turned = pltpu.roll(acc[b], PER, 1)
                even = jnp.where(first_half, acc[b], pltpu.roll(turned, 4, 0))
                odd = jnp.where(first_half, turned, pltpu.roll(acc[b], 4, 0))
                out_ref[2 * c, b] = even[:4]
                out_ref[2 * c + 1, b] = odd[:4]
        if pair % 2:
            peers = pl.ds(4 * pair - 4, 8)
            copies.append(
                pltpu.make_async_copy(out_ref.at[peers], out_hbm.at[peers], done.at[pair // 2])
            )
            copies[-1].start()
    for copy in copies:
        copy.wait()


def reply(coef, got):
    return pl.pallas_call(
        reply_kernel,
        out_shape=jax.ShapeDtypeStruct((PEERS, BLOCKS, 4, ELEM), jnp.float32),
        in_specs=[VMEM, VMEM],
        out_specs=pl.BlockSpec(memory_space=pl.ANY),
        scratch_shapes=[
            pltpu.VMEM((2 * LEV, COLS), jnp.bfloat16),
            pltpu.VMEM((PEERS, BLOCKS, 4, ELEM), jnp.float32),
            pltpu.SemaphoreType.DMA((4,)),
        ],
        compiler_params=PARAMS,
        cost_estimate=cost(2.4),
        name="reply",
    )(inside(coef), inside(got))


TABLE = 5 * ELEM


def fill_edges(edges, point):
    for t in range(4):
        for s in range(4):
            edges[t * LEV : (t + 1) * LEV, s * ELEM : (s + 1) * ELEM] = point(EDGE_POINT[s][t])


def turn(value, lanes):
    lanes = lanes % ELEM
    return pltpu.roll(value, lanes, 1) if lanes else value


def emit(edges, chosen, row_ref, east_ref, west_ref):
    out = moved(parts_of(edges[:, : 4 * ELEM]), one_hot(chosen, 4 * ELEM))
    out = [out[t * LEV : (t + 1) * LEV] for t in range(4)]
    lane = iota((LEV, ELEM), 1)
    value = out[0]
    for t in range(1, 4):
        value = jnp.where((lane >> 5) == t, turn(out[t], 32 * t), value)
    row_ref[...] = value
    lane24 = iota((THIRD, ELEM), 1)
    for start, ref in ((2 * BC, east_ref), (2 * BC + BR, west_ref)):
        value = turn(out[0], -start)
        for t in range(1, 4):
            value = jnp.where((lane >> 3) == t, turn(out[t], 8 * t - start), value)
        packed = value[:THIRD]
        for j in range(1, 3):
            block = turn(value[j * THIRD : (j + 1) * THIRD], 32 * j)
            packed = jnp.where((lane24 >> 5) == j, block, packed)
        ref[...] = packed


THIRD = LEV // 3
FLAT = pltpu.VMEM((LEV, ELEM), jnp.float32)
SIDE = pltpu.VMEM((THIRD, ELEM), jnp.float32)


def route(span_slot, nbr_slot, edge_flip, send_slot, metric):
    return pl.pallas_call(
        route_kernel,
        out_shape=(
            pltpu.VMEM((PEERS, 1, ELEM), jnp.int32),
            pltpu.VMEM((PTS, ELEM), jnp.int32),
            pltpu.VMEM((16, ELEM), jnp.int32),
            pltpu.VMEM((8, ELEM), jnp.float32),
        ),
        in_specs=[VMEM] * 5,
        out_specs=(VMEM,) * 4,
        compiler_params=PARAMS,
        cost_estimate=cost(1.2),
        name="route",
    )(*[outside(x) for x in (span_slot, nbr_slot, edge_flip, send_slot.reshape(1, -1), metric.reshape(1, ELEM))])


def halo_kernel(tracer_ref, table_ref, row_ref, east_ref, west_ref, edges):
    fill_edges(edges, lambda p: tracer_ref[pl.ds(p, LEV, stride=PTS), :])
    emit(edges, table_ref[8:9, :], row_ref, east_ref, west_ref)


def halo(tracer, table):
    return pl.pallas_call(
        halo_kernel,
        out_shape=(FLAT, SIDE, SIDE),
        in_specs=[VMEM, VMEM],
        out_specs=(VMEM,) * 3,
        scratch_shapes=[pltpu.VMEM((4 * LEV, 4 * ELEM), jnp.float32)],
        compiler_params=PARAMS,
        cost_estimate=cost(1.0),
        name="halo",
    )(inside(tracer), inside(table))


def received(incoming):
    below, above, west, east = [ref[...] for ref in incoming]
    lane = iota((LEV, ELEM), 1)
    lane24 = iota((THIRD, ELEM), 1)
    row_in = jnp.where((lane & 31) < BC, below, above)
    result = []
    for t in range(4):
        sides = [
            jnp.where(
                lane24 < 2 * BC + BR,
                turn(west, 2 * BC - (32 * j + 8 * t)),
                turn(east, 2 * BC + BR - (32 * j + 8 * t)),
            )
            for j in range(3)
        ]
        sides = jnp.concatenate(sides, axis=0)
        result.append(jnp.where(lane < 2 * BC, turn(row_in, -32 * t), sides))
    return result


def neighbours(table_ref):
    return jnp.concatenate([table_ref[s : s + 1, :] for s in range(4)], axis=1)


def edge_sums(across, turned, b):
    sums = [None] * PTS
    for s in range(4):
        raw = [
            across[pl.ds(pl.multiple_of(t * LEV + b * 8, 8), 8), s * ELEM : (s + 1) * ELEM]
            for t in range(4)
        ]
        for t in range(4):
            p = EDGE_POINT[s][t]
            value = jnp.where(turned[s], raw[3 - t], raw[t])
            sums[p] = value if sums[p] is None else sums[p] + value
    return sums


def operator(slabs, metric, turned, across, b):
    stiff = stiffness()
    edge_sum = edge_sums(across, turned, b)
    result = []
    for i in range(4):
        for j in range(4):
            p = 4 * i + j
            edges = (i in (0, 3)) + (j in (0, 3))
            total = slabs[p] * float(stiff[i, i] + stiff[j, j] - PENALTY * edges)
            for q in range(4):
                if q != i:
                    total = total + slabs[4 * q + j] * float(stiff[i, q])
                if q != j:
                    total = total + slabs[4 * i + q] * float(stiff[j, q])
            if edges:
                total = total + PENALTY * edge_sum[p]
            result.append(metric * total)
    return result


def turned_of(table_ref):
    return [jnp.broadcast_to(table_ref[s : s + 1, :], (8, ELEM)) == 1 for s in range(4, 8)]


def first_kernel(
    tracer_ref, metric_ref, table_ref, below_ref, above_ref, west_ref, east_ref,
    first_ref, row_ref, east_out, west_out, edges, across,
):
    fill_edges(edges, lambda p: tracer_ref[pl.ds(p, LEV, stride=PTS), :])
    halo_in = received((below_ref, above_ref, west_ref, east_ref))
    for t in range(4):
        edges[t * LEV : (t + 1) * LEV, 4 * ELEM :] = halo_in[t]
    across[...] = moved(parts_of(edges[...]), one_hot(neighbours(table_ref), TABLE))
    metric = metric_ref[...]

    def block(b, carry):
        at = pl.ds(pl.multiple_of(b * 8, 8), 8)
        slabs = [tracer_ref[pl.ds(b * (8 * PTS) + p, 8, stride=PTS), :] for p in range(PTS)]
        result = operator(slabs, metric, turned_of(table_ref), across, b)
        for p in range(PTS):
            first_ref[p, at, :] = result[p]
        return carry

    lax.fori_loop(0, BLOCKS, block, 0, unroll=True)
    fill_edges(edges, lambda p: first_ref[p])
    emit(edges, table_ref[8:9, :], row_ref, east_out, west_out)


EDGE_SCRATCH = [
    pltpu.VMEM((4 * LEV, TABLE), jnp.float32),
    pltpu.VMEM((4 * LEV, 4 * ELEM), jnp.float32),
]


def first_pass(tracer, metric, table, incoming):
    return pl.pallas_call(
        first_kernel,
        out_shape=(pltpu.VMEM((PTS, LEV, ELEM), jnp.float32), FLAT, SIDE, SIDE),
        in_specs=[VMEM] * 7,
        out_specs=(VMEM,) * 4,
        scratch_shapes=EDGE_SCRATCH,
        compiler_params=PARAMS,
        cost_estimate=cost(2.4),
        name="first_pass",
    )(*[inside(x) for x in (tracer, metric, table, *incoming)])


def second_kernel(tracer_ref, field_ref, metric_ref, table_ref, stepped_ref, edges, across):
    fill_edges(edges, lambda p: field_ref[p])
    across[...] = moved(parts_of(edges[...]), one_hot(neighbours(table_ref), 4 * ELEM))
    metric = metric_ref[...]

    def block(b, carry):
        at = pl.ds(pl.multiple_of(b * 8, 8), 8)
        slabs = [field_ref[p, at, :] for p in range(PTS)]
        result = operator(slabs, metric, turned_of(table_ref), across, b)
        for p in range(PTS):
            point = pl.ds(b * (8 * PTS) + p, 8, stride=PTS)
            stepped_ref[point, :] = tracer_ref[point, :] - HYPER * result[p]
        return carry

    lax.fori_loop(0, BLOCKS, block, 0, unroll=True)


def second_pass(tracer, field, metric, table):
    return pl.pallas_call(
        second_kernel,
        out_shape=pltpu.VMEM((LEV * PTS, ELEM), jnp.float32),
        in_specs=[VMEM] * 4,
        out_specs=VMEM,
        scratch_shapes=[pltpu.VMEM((4 * LEV, 4 * ELEM), jnp.float32)] * 2,
        compiler_params=PARAMS,
        cost_estimate=cost(1.2),
        name="second_pass",
    )(*[inside(x) for x in (tracer, field, metric, table)])


def finish_kernel(
    partial_ref, metric_ref, table_ref, below_ref, above_ref, west_ref, east_ref, stepped_ref, across
):
    halo_in = jnp.concatenate(received((below_ref, above_ref, west_ref, east_ref)), axis=0)
    across[...] = moved(parts_of(halo_in), one_hot(neighbours(table_ref) - 4 * ELEM, ELEM))
    weight = (HYPER * PENALTY) * metric_ref[...]

    def block(b, carry):
        sums = edge_sums(across, turned_of(table_ref), b)
        for p in range(PTS):
            point = pl.ds(b * (8 * PTS) + p, 8, stride=PTS)
            value = partial_ref[point, :]
            stepped_ref[point, :] = value if sums[p] is None else value - weight * sums[p]
        return carry

    lax.fori_loop(0, BLOCKS, block, 0, unroll=True)


def finish(partial, metric, table, incoming):
    return pl.pallas_call(
        finish_kernel,
        out_shape=pltpu.VMEM((LEV * PTS, ELEM), jnp.float32),
        in_specs=[VMEM] * 7,
        out_specs=VMEM,
        scratch_shapes=[pltpu.VMEM((4 * LEV, 4 * ELEM), jnp.float32)],
        compiler_params=PARAMS,
        cost_estimate=cost(0.7),
        name="finish",
    )(*[inside(x) for x in (partial, metric, table, *incoming)])


def mix_kernel(reply_ref, bucket_ref, stepped_ref, out_ref, wide, data, mixing, gain, carried, base, link, right):
    first_half = iota((4, ELEM), 1) < PER
    for c in range(PTS):
        lanes = slice(c * ELEM, (c + 1) * ELEM)
        for b in range(BLOCKS):
            even, odd = reply_ref[2 * c, b], reply_ref[2 * c + 1, b]
            low = jnp.where(first_half, even, pltpu.roll(odd, PER, 1))
            high = jnp.where(first_half, pltpu.roll(even, PER, 1), odd)
            wide[8 * b : 8 * b + 8, lanes] = jnp.concatenate([low, high], axis=0)
    data[...] = parts_of(wide[...])
    for p in range(0, PTS, 2):
        index = jnp.concatenate([bucket_ref[p : p + 1, :], bucket_ref[p + 1 : p + 2, :]], axis=1)
        value = moved(data[...], one_hot(index, COLS))
        for u in range(2):
            mixing[pl.ds(p + u, LEV, stride=PTS), :] = value[:, u * ELEM : (u + 1) * ELEM]

    def level(ref, k):
        return ref[k * PTS : (k + 1) * PTS, :]

    def keep(ref, k, value):
        ref[k * PTS : (k + 1) * PTS, :] = value

    high = level(mixing, 0)
    carry = jnp.zeros((PTS, ELEM), jnp.float32)
    for k in range(1, LEV, 2):
        here = level(mixing, k)
        last = k == LEV - 1
        scale = 1.0 / (1.0 + here if last else 1.0 + here + level(mixing, k + 1))
        moved_here = level(stepped_ref, k) * scale
        low = here * scale
        keep(base, k - 1, 1.0 + high + low)
        keep(right, k - 1, level(stepped_ref, k - 1) + carry + here * moved_here)
        keep(base, k, low)
        keep(right, k, moved_here)
        if not last:
            after = level(mixing, k + 1)
            high = after * scale
            carry = after * moved_here
            keep(link, k, high)
            keep(link, k + 1, high * here)

    half = LEV // 4
    up_gain = down_gain = up_rhs = down_rhs = None
    for i in range(half):
        k = 2 * i
        after = level(link, k + 2)
        total = level(base, k) + after
        value = level(right, k)
        if i:
            here = level(link, k)
            total = total + here * (1.0 - up_gain)
            value = value + here * up_rhs
        scale = 1.0 / total
        up_rhs, up_gain = value * scale, after * scale
        m = LEV - 2 - k
        here = level(link, m)
        total = level(base, m) + here
        value = level(right, m)
        if i:
            after = level(link, m + 2)
            total = total + after * (1.0 - down_gain)
            value = value + after * down_rhs
        scale = 1.0 / total
        down_rhs, down_gain = value * scale, here * scale
        if i < half - 1:
            for at, one, two in ((k, up_gain, up_rhs), (m, down_gain, down_rhs)):
                keep(gain, at, one)
                keep(carried, at, two)
    upper = (up_rhs + up_gain * down_rhs) / (1.0 - up_gain * down_gain)
    lower = down_rhs + down_gain * upper
    middle = LEV // 2 - 2
    out_ref[middle] = upper
    out_ref[middle + 2] = lower
    out_ref[middle + 1] = (
        level(right, middle + 1) + level(base, middle + 1) * upper + level(link, middle + 1) * lower
    )
    for k in range(middle - 2, -1, -2):
        below = level(carried, k) + level(gain, k) * upper
        out_ref[k] = below
        out_ref[k + 1] = level(right, k + 1) + level(base, k + 1) * below + level(link, k + 1) * upper
        upper = below
        m = LEV - 2 - k
        above = level(carried, m) + level(gain, m) * lower
        out_ref[m] = above
        out_ref[m - 1] = level(right, m - 1) + level(base, m - 1) * lower + level(link, m - 1) * above
        lower = above
    end = LEV - 1
    out_ref[end] = level(right, end) + level(base, end) * lower


def mix(replied, bucket, stepped):
    rows = LEV * PTS
    return pl.pallas_call(
        mix_kernel,
        out_shape=jax.ShapeDtypeStruct((LEV, PTS, ELEM), jnp.float32),
        in_specs=[VMEM] * 3,
        out_specs=VMEM,
        scratch_shapes=[
            pltpu.VMEM((LEV, COLS), jnp.float32),
            pltpu.VMEM((2 * LEV, COLS), jnp.bfloat16),
        ]
        + [pltpu.VMEM((rows, ELEM), jnp.float32)] * 6,
        compiler_params=PARAMS,
        cost_estimate=cost(2.8),
        name="mix",
    )(*[inside(x) for x in (replied, bucket, stepped)])


def exchange(row_out, east_out, west_out):
    def moved_by(value, axis, step):
        size = lax.axis_size(axis)
        return lax.ppermute(value, axis, [(i, (i + step) % size) for i in range(size)])

    return (
        moved_by(row_out, "grp", 1),
        moved_by(row_out, "grp", -1),
        moved_by(east_out, "dev", 1),
        moved_by(west_out, "dev", -1),
    )


def on_device(tracer, metric, coef, nbr_slot, edge_flip, send_slot, span_slot):
    flat = tracer.reshape(LEV * PTS, ELEM)
    asked, bucket, table, metric = route(span_slot, nbr_slot, edge_flip, send_slot, metric)
    outgoing = halo(flat, table)
    got = lax.all_to_all(asked, "dev", split_axis=0, concat_axis=0, tiled=True)
    incoming = exchange(*outgoing)
    replied = lax.all_to_all(reply(coef, got), "dev", split_axis=0, concat_axis=0, tiled=True)
    first, *outgoing = first_pass(flat, metric, table, incoming)
    partial = second_pass(flat, first, metric, table)
    stepped = finish(partial, metric, table, exchange(*outgoing))
    return mix(replied, bucket, stepped)


def solution(mesh):
    in_specs = (
        P(None, None, ("grp", "dev")),
        P(("grp", "dev")),
        P(None, ("grp", "dev")),
        P(None, ("grp", "dev")),
        P(None, ("grp", "dev")),
        P(("grp", "dev")),
        P(None, ("grp", "dev")),
    )
    out_specs = P(None, None, ("grp", "dev"))
    return jax.shard_map(
        on_device, mesh=mesh, in_specs=in_specs, out_specs=out_specs, check_vma=False
    )
```
